128 devices in a mesh: ctx: 16 (over z_lo, y, core), ulys: 8 (over z_hi, x).
Axes of the slice: x: 4, y: 4, z: 4 (z_hi: 2, z_lo: 2; z = z_hi * 2 + z_lo), core: 2. Of those that a mesh axis runs over, the one named last changes fastest.
Arguments:
- queries: bfloat16 [32768, 2048], P(('ctx', 'ulys')), may hold values from -32 to 32
- keys: bfloat16 [32768, 2048], P(('ctx', 'ulys')), may hold values from -32 to 32
- values: bfloat16 [32768, 2048], P(('ctx', 'ulys')), may hold values from -6 to 6
- rand_blocks: int32 [512, 3], replicated, may hold values from 0 to 511, as said below
- out_weight: bfloat16 [2048, 4096], replicated, may hold values from -0.125 to 0.125
Outputs:
- output: bfloat16 [32768, 4096], P(('ctx', 'ulys'))
The draws below stay inside these ranges and needn't reach their ends.
Inputs may be any that keep to these rules, and one draw needn't show every extreme that they name: `rand_blocks`: for the query blocks of one context group (rows 32 * c to 32 * c + 31), at most 12 of their random entries name blocks of any one group (blocks 32 * e to 32 * e + 31); every group's query blocks reach 12 for some group e.
All inputs are finite; a program needn't handle non-finite values.
Results may differ from the reference program's by a relative error of at most 0.0057.
Values may be sent and summed in bfloat16 or wider, within the bound.
A program may use at most 192 MiB of HBM per device.

```python
import jax
import jax.numpy as jnp
from jax import lax

H = 16
DH = 128
D = 4096
BLK = 64
GLOB = 2
RAND = 3
TOKENS = 32768
QBG = 32
NB = 512
CAP = 12


def draw_queries(key, part):
    own_key = jax.random.fold_in(key, 11)
    filled = jnp.clip(jax.random.normal(own_key, (TOKENS, H * DH), jnp.float32), -6.0, 6.0)
    return filled.astype(jnp.bfloat16)


def draw_keys(key, part):
    own_key = jax.random.fold_in(key, 13)
    filled = jnp.clip(jax.random.normal(own_key, (TOKENS, H * DH), jnp.float32), -6.0, 6.0)
    return filled.astype(jnp.bfloat16)


def draw_rand_blocks(key, part):
    group_total = NB // QBG
    share = CAP // 2
    pair_count = max((group_total - 2) // 2, 1)
    slot_total = group_total * share

    def one_reader(reader_key):
        perm_key, split_key, within_key, order_key = jax.random.split(reader_key, 4)
        owners_perm = jax.random.permutation(perm_key, group_total).astype(jnp.int32)
        splits = jax.random.randint(split_key, (pair_count,), 0, 2 * share + 1, dtype=jnp.int32)
        slots = jnp.arange(slot_total, dtype=jnp.int32)
        shifted = slots - 2 * share
        pair_idx = jnp.clip(shifted // (2 * share), 0, pair_count - 1)
        within_pair = shifted % (2 * share)
        rank = jnp.where(slots < 2 * share, 0, jnp.where(within_pair < splits[pair_idx], 1 + 2 * pair_idx, 2 + 2 * pair_idx))
        owner = owners_perm[rank]
        within = jax.random.randint(within_key, (slot_total,), 0, QBG, dtype=jnp.int32)
        blocks = owner * QBG + within
        order = jax.random.permutation(order_key, slot_total)
        return blocks[order].reshape(QBG, RAND)
    reader_keys = jax.random.split(jax.random.fold_in(key, 17), group_total)
    return jax.vmap(one_reader)(reader_keys).reshape(NB, RAND).astype(jnp.int32)


def block_levels(stream_key, shape, cuts, low, high):
    def one(dim, shards_of):
        steps = jax.random.uniform(jax.random.fold_in(jax.random.fold_in(stream_key, 6), dim), (shards_of,), jnp.float32, low / len(cuts), high / len(cuts))
        return jnp.repeat(jnp.exp(steps), shape[dim] // shards_of).reshape((-1,) + (1,) * (len(shape) - dim - 1))

    loudness = one(*cuts[0])
    for cut in cuts[1:]:
        loudness = loudness * one(*cut)
    return loudness


def normal_values(key, shape, spread, reach, cuts=(), kind=jnp.bfloat16):
    drawn = jax.random.normal(key, shape, jnp.float32) * spread
    if len(cuts) > 0:
        drawn = block_levels(key, shape, cuts, -0.22, 0.18) * drawn
    return jnp.clip(drawn, min=-reach, max=reach).astype(kind)


def setup_inputs(seed: int = 0) -> dict:
    streams_of = jax.random.split(jax.random.key(seed), 6)
    return {
        "queries": draw_queries(jax.random.fold_in(streams_of[5], 71), 0),
        "keys": draw_keys(jax.random.fold_in(streams_of[5], 71), 0),
        "values": normal_values(streams_of[2], (TOKENS, H * DH), 1.0, 6.0, ((0, 128),)),
        "rand_blocks": draw_rand_blocks(jax.random.fold_in(streams_of[5], 71), 0),
        "out_weight": normal_values(streams_of[4], (H * DH, D), (H * DH) ** -0.5, 0.125),
    }


def reference(queries, keys, values, rand_blocks, out_weight):
    block_ids = jnp.arange(NB, dtype=jnp.int32)
    window = jnp.stack([(block_ids - 1) % NB, block_ids, (block_ids + 1) % NB], axis=1)
    leading = jnp.broadcast_to(jnp.arange(GLOB, dtype=jnp.int32)[None, :], (NB, GLOB))
    table = jnp.concatenate([window, leading, rand_blocks.astype(jnp.int32)], axis=1)
    query_blocks = queries.reshape(NB, BLK, H, DH)
    key_blocks = keys.reshape(NB, BLK, H, DH)
    value_blocks = values.reshape(NB, BLK, H, DH)
    group_count = NB // QBG

    def one_group(index):
        first = (index * QBG).astype(jnp.int32)
        rows = lax.dynamic_slice_in_dim(table, first, QBG, 0)
        query_grp = lax.dynamic_slice_in_dim(query_blocks, first, QBG, 0).astype(jnp.float32)
        key_grp = key_blocks[rows].reshape(QBG, -1, H, DH).astype(jnp.float32)
        value_grp = value_blocks[rows].reshape(QBG, -1, H, DH).astype(jnp.float32)
        scores = jnp.einsum("bqhd,bkhd->bhqk", query_grp, key_grp) * (DH ** -0.5)
        peak_score = jnp.max(scores, axis=-1, keepdims=True)
        lifted = jnp.exp(scores - peak_score)
        weights = (lifted / jnp.sum(lifted, axis=-1, keepdims=True)).astype(jnp.bfloat16)
        weights = lax.optimization_barrier(weights).astype(jnp.float32)
        attended = jnp.einsum("bhqk,bkhd->bqhd", weights, value_grp).astype(jnp.bfloat16)
        return attended.reshape(QBG * BLK, H * DH)

    attended = lax.map(one_group, jnp.arange(group_count, dtype=jnp.int32)).reshape(TOKENS, H * DH)
    return jnp.dot(attended, out_weight, preferred_element_type=jnp.float32).astype(jnp.bfloat16)
```

```python
import functools

import jax
import jax.numpy as jnp
from jax import lax
from jax.experimental import pallas as pl
from jax.experimental.pallas import tpu as pltpu
from jax.sharding import PartitionSpec as P

H = 16
DH = 128
D = 4096
BLK = 64
NB = 512
TOKENS = 32768
SHARE = 256
MESH = pl.DeviceIdType.MESH
LAG = 2
LAG_FAR = 4
TILE_N = 512
EXP_SCALE = (DH ** -0.5) * 1.4426950408889634


def mesh_id(x, y, z, core):
    return ((lax.rem(z, 2) * 4 + y) * 2 + core, lax.div(z, 2) * 4 + x)


def token_share(x, y, z, core):
    ctx, ulys = mesh_id(x, y, z, core)
    return ctx * 8 + ulys


def kernel(rand, q_in, k_in, v_in, w_in, out,
           kv, qb, ob, att, wv, outv,
           own_sem, s1_send, s1_recv, q_recv, up_recv, dn_recv, far_recv,
           ring_send, sib_send, sib_recv, ret_send, ret_recv, w_sem, out_sem):
    ctx, ulys = lax.axis_index("ctx"), lax.axis_index("ulys")
    core = lax.rem(ctx, 2)
    y = lax.rem(lax.div(ctx, 2), 4)
    z = lax.div(ulys, 4) * 2 + lax.div(ctx, 8)
    x = lax.rem(ulys, 4)
    head = y * 4 + x
    z_up, z_dn, z_far = lax.rem(z + 1, 4), lax.rem(z + 3, 4), lax.rem(z + 2, 4)
    up, dn = mesh_id(x, y, z_up, core), mesh_id(x, y, z_dn, core)
    sib = mesh_id(x, y, z, 1 - core)

    def peer(k):
        return lax.rem(x + lax.rem(k, 4), 4), lax.rem(y + lax.div(k, 4), 4)

    def back(k):
        return lax.rem(x + 4 - lax.rem(k, 4), 4), lax.rem(y + 4 - lax.div(k, 4), 4)

    def lanes(h):
        return pl.ds(pl.multiple_of(h * DH, DH), DH)

    def rows(k, zz):
        px, py = peer(k)
        return pl.ds(token_share(px, py, zz, core) * 4, 4)

    my_rows = rows(0, z)
    w_copies = [
        pltpu.make_async_copy(w_in.at[pl.ds(i * 256, 256)], wv.at[pl.ds(i * 256, 256)], w_sem.at[i])
        for i in range(8)
    ]
    own = [
        pltpu.make_async_copy(k_in.at[:, :, lanes(head)], kv.at[0, my_rows], own_sem.at[0]),
        pltpu.make_async_copy(v_in.at[:, :, lanes(head)], kv.at[1, my_rows], own_sem.at[1]),
        pltpu.make_async_copy(q_in.at[:, lanes(head)], qb.at[pl.ds(0, SHARE)], own_sem.at[2]),
    ]
    for copy in own:
        copy.start()

    barrier = pltpu.get_barrier_semaphore()
    for device in (up, dn, sib):
        pl.semaphore_signal(barrier, inc=1, device_id=device, device_id_type=MESH)

    @pl.loop(1, 16)
    def _(k):
        px, py = back(k)
        pl.semaphore_signal(barrier, inc=1, device_id=mesh_id(px, py, z, core), device_id_type=MESH)

    pl.semaphore_wait(barrier, 18)

    def remote(src, dst, send, recv, device):
        return pltpu.make_async_remote_copy(
            src_ref=src, dst_ref=dst, send_sem=send, recv_sem=recv,
            device_id=device, device_id_type=MESH)

    @pl.loop(1, 16)
    def _(k):
        px, py = back(k)
        device = mesh_id(px, py, z, core)
        h = py * 4 + px
        remote(k_in.at[:, :, lanes(h)], kv.at[0, my_rows], s1_send.at[0], s1_recv.at[k], device).start()
        remote(v_in.at[:, :, lanes(h)], kv.at[1, my_rows], s1_send.at[1], s1_recv.at[k], device).start()

    @pl.loop(1, 16)
    def _(k):
        px, py = back(k)
        device = mesh_id(px, py, z, core)
        h = py * 4 + px
        slot = pl.ds(pl.multiple_of(k * SHARE, SHARE), SHARE)
        remote(q_in.at[:, lanes(h)], qb.at[slot], s1_send.at[2], q_recv, device).start()

    for copy in w_copies:
        copy.start()
    own[0].wait()
    own[1].wait()

    def wait_piece(piece, sem):
        pltpu.make_async_copy(piece, piece, sem).wait()

    def push(piece, send, recv, device):
        remote(piece, piece, send, recv, device).start()

    def spread(k):
        piece = kv.at[:, rows(k, z)]

        @pl.when(k > 0)
        def _():
            wait_piece(piece, s1_recv.at[k])
        push(piece, ring_send.at[0], up_recv.at[k], up)
        push(piece, ring_send.at[1], dn_recv.at[k], dn)
        push(piece, sib_send.at[0], sib_recv.at[0], sib)

    def relay(k):
        low = kv.at[:, rows(k, z_dn)]
        high = kv.at[:, rows(k, z_up)]
        wait_piece(low, up_recv.at[k])

        @pl.when(lax.rem(k, 2) == 0)
        def _():
            push(low, ring_send.at[2], far_recv.at[k], up)
        push(low, sib_send.at[1], sib_recv.at[1], sib)
        wait_piece(high, dn_recv.at[k])

        @pl.when(lax.rem(k, 2) == 1)
        def _():
            push(high, ring_send.at[3], far_recv.at[k], dn)
        push(high, sib_send.at[2], sib_recv.at[2], sib)

    def last(k):
        piece = kv.at[:, rows(k, z_far)]
        wait_piece(piece, far_recv.at[k])
        push(piece, sib_send.at[3], sib_recv.at[3], sib)

    @pl.loop(0, 16 + LAG_FAR)
    def _(i):
        @pl.when(i < 16)
        def _():
            spread(i)

        @pl.when((i >= LAG) & (i < 16 + LAG))
        def _():
            relay(i - LAG)

        @pl.when(i >= LAG_FAR)
        def _():
            last(i - LAG_FAR)

    own[2].wait()
    wait_piece(qb.at[pl.ds(0, 15 * SHARE)], q_recv)
    span = kv.at[:, pl.ds(0, 64)]
    for i in range(4):
        wait_piece(span, sib_recv.at[i])

    @pl.loop(0, 16)
    def _(k):
        px, py = peer(k)
        first = token_share(px, py, z, core) * 4
        outs = []
        for j in range(4):
            b = first + j
            picks = [
                lax.rem(b + NB - 1, NB), b, lax.rem(b + 1, NB), 0, 1,
                rand[b, 0], rand[b, 1], rand[b, 2],
            ]

            def listed(side):
                parts = []
                for pick in picks:
                    parts.append(kv[side, pick])
                return jnp.concatenate(parts, axis=0)

            q = qb[pl.ds(pl.multiple_of(k * SHARE + j * BLK, BLK), BLK), :]
            s = lax.dot_general(q, listed(0), (((1,), (1,)), ((), ())), preferred_element_type=jnp.float32)
            peak = jnp.max(s, axis=-1, keepdims=True)
            lifted = jnp.exp2((s - peak) * EXP_SCALE)
            total = jnp.sum(lifted, axis=-1, keepdims=True)
            weights = (lifted / total).astype(jnp.bfloat16)
            outs.append(jnp.dot(weights, listed(1), preferred_element_type=jnp.float32).astype(jnp.bfloat16))
        slot = pl.ds(pl.multiple_of(k * SHARE, SHARE), SHARE)
        ob[slot, :] = jnp.concatenate(outs, axis=0)

        @pl.when(k > 0)
        def _():
            remote(ob.at[slot], att.at[:, lanes(head)], ret_send, ret_recv, mesh_id(px, py, z, core)).start()

    keep = pltpu.make_async_copy(ob.at[pl.ds(0, SHARE)], att.at[:, lanes(head)], own_sem.at[0])
    keep.start()
    for copy in w_copies:
        copy.wait()
    keep.wait()
    fifteen = ob.at[pl.ds(0, 15 * SHARE)]
    wait_piece(fifteen, ret_recv)

    @pl.loop(0, D // TILE_N)
    def _(n):
        cols = pl.ds(pl.multiple_of(n * TILE_N, TILE_N), TILE_N)
        outv[:, cols] = jnp.dot(att[...], wv[:, cols], preferred_element_type=jnp.float32).astype(jnp.bfloat16)
        pltpu.make_async_copy(outv.at[:, cols], out.at[:, cols], out_sem).start()

    wait_piece(outv, out_sem)
    wait_piece(fifteen, ret_send)
    for i in range(3):
        wait_piece(fifteen, s1_send.at[i])
    for i in range(2):
        wait_piece(span, ring_send.at[i])
    half = kv.at[:, pl.ds(0, 32)]
    for i in range(2, 4):
        wait_piece(half, ring_send.at[i])
    for i in range(4):
        wait_piece(span, sib_send.at[i])


def shards(queries, keys, values, rand_blocks, out_weight):
    any_spec = pl.BlockSpec(memory_space=pl.ANY)
    dma = pltpu.SemaphoreType.DMA
    return pl.pallas_call(
        kernel,
        out_shape=jax.ShapeDtypeStruct((SHARE, D), jnp.bfloat16),
        in_specs=[pl.BlockSpec(memory_space=pltpu.SMEM)] + [any_spec] * 4,
        out_specs=any_spec,
        scratch_shapes=[
            pltpu.VMEM((2, NB, BLK, DH), jnp.bfloat16),
            pltpu.VMEM((16 * SHARE, DH), jnp.bfloat16),
            pltpu.VMEM((16 * SHARE, DH), jnp.bfloat16),
            pltpu.VMEM((SHARE, H * DH), jnp.bfloat16),
            pltpu.VMEM((H * DH, D), jnp.bfloat16),
            pltpu.VMEM((SHARE, D), jnp.bfloat16),
            dma((3,)), dma((3,)), dma((16,)), dma, dma((16,)), dma((16,)), dma((16,)),
            dma((4,)), dma((4,)), dma((4,)), dma, dma, dma((8,)), dma,
        ],
        compiler_params=pltpu.CompilerParams(
            collective_id=0, has_side_effects=True, vmem_limit_bytes=56 * 1024 * 1024),
    )(rand_blocks, queries, keys.reshape(4, BLK, H * DH), values.reshape(4, BLK, H * DH), out_weight)


def solution(mesh):
    return jax.shard_map(
        shards,
        mesh=mesh,
        in_specs=(
            P(("ctx", "ulys"), None),
            P(("ctx", "ulys"), None),
            P(("ctx", "ulys"), None),
            P(),
            P(),
        ),
        out_specs=P(("ctx", "ulys"), None),
        check_vma=False,
    )
```

```python
import functools

import jax
import jax.numpy as jnp
from jax import lax
from jax.experimental import pallas as pl
from jax.experimental.pallas import tpu as pltpu
from jax.sharding import PartitionSpec as P

H = 16
DH = 128
D = 4096
BLK = 64
NB = 512
TOKENS = 32768
SHARE = 256
MESH = pl.DeviceIdType.MESH
LAG = 2
LAG_FAR = 4
TILE_N = 512
GANG = 2
EXP_SCALE = (DH ** -0.5) * 1.4426950408889634


def mesh_id(x, y, z, core):
    return ((lax.rem(z, 2) * 4 + y) * 2 + core, lax.div(z, 2) * 4 + x)


def token_share(x, y, z, core):
    ctx, ulys = mesh_id(x, y, z, core)
    return ctx * 8 + ulys


def kernel(rand, q_in, k_in, v_in, w_in, out,
           kv, qb, ob, att, wv, outv,
           own_sem, s1_send, s1_recv, q_recv, up_recv, dn_recv, far_recv,
           ring_send, sib_send, sib_recv, ret_send, ret_recv, w_sem, out_sem):
    ctx, ulys = lax.axis_index("ctx"), lax.axis_index("ulys")
    core = lax.rem(ctx, 2)
    y = lax.rem(lax.div(ctx, 2), 4)
    z = lax.div(ulys, 4) * 2 + lax.div(ctx, 8)
    x = lax.rem(ulys, 4)
    head = y * 4 + x
    z_up, z_dn, z_far = lax.rem(z + 1, 4), lax.rem(z + 3, 4), lax.rem(z + 2, 4)
    up, dn = mesh_id(x, y, z_up, core), mesh_id(x, y, z_dn, core)
    sib = mesh_id(x, y, z, 1 - core)

    def peer(k):
        return lax.rem(x + lax.rem(k, 4), 4), lax.rem(y + lax.div(k, 4), 4)

    def back(k):
        return lax.rem(x + 4 - lax.rem(k, 4), 4), lax.rem(y + 4 - lax.div(k, 4), 4)

    def lanes(h):
        return pl.ds(pl.multiple_of(h * DH, DH), DH)

    def rows(k, zz):
        px, py = peer(k)
        return pl.ds(token_share(px, py, zz, core) * 4, 4)

    my_rows = rows(0, z)
    w_copies = [
        pltpu.make_async_copy(w_in.at[pl.ds(i * 256, 256)], wv.at[pl.ds(i * 256, 256)], w_sem.at[i])
        for i in range(8)
    ]
    own = [
        pltpu.make_async_copy(k_in.at[:, :, lanes(head)], kv.at[0, my_rows], own_sem.at[0]),
        pltpu.make_async_copy(v_in.at[:, :, lanes(head)], kv.at[1, my_rows], own_sem.at[1]),
        pltpu.make_async_copy(q_in.at[:, lanes(head)], qb.at[pl.ds(0, SHARE)], own_sem.at[2]),
    ]
    for copy in own:
        copy.start()

    barrier = pltpu.get_barrier_semaphore()
    for device in (up, dn, sib):
        pl.semaphore_signal(barrier, inc=1, device_id=device, device_id_type=MESH)

    @pl.loop(1, 16)
    def _(k):
        px, py = back(k)
        pl.semaphore_signal(barrier, inc=1, device_id=mesh_id(px, py, z, core), device_id_type=MESH)

    pl.semaphore_wait(barrier, 18)

    def remote(src, dst, send, recv, device):
        return pltpu.make_async_remote_copy(
            src_ref=src, dst_ref=dst, send_sem=send, recv_sem=recv,
            device_id=device, device_id_type=MESH)

    @pl.loop(1, 16)
    def _(k):
        px, py = back(k)
        device = mesh_id(px, py, z, core)
        h = py * 4 + px
        remote(k_in.at[:, :, lanes(h)], kv.at[0, my_rows], s1_send.at[0], s1_recv.at[k], device).start()
        remote(v_in.at[:, :, lanes(h)], kv.at[1, my_rows], s1_send.at[1], s1_recv.at[k], device).start()

    @pl.loop(1, 16)
    def _(k):
        px, py = back(k)
        device = mesh_id(px, py, z, core)
        h = py * 4 + px
        slot = pl.ds(pl.multiple_of(k * SHARE, SHARE), SHARE)
        remote(q_in.at[:, lanes(h)], qb.at[slot], s1_send.at[2], q_recv, device).start()

    for copy in w_copies:
        copy.start()
    own[0].wait()
    own[1].wait()

    def wait_piece(piece, sem):
        pltpu.make_async_copy(piece, piece, sem).wait()

    def push(piece, send, recv, device):
        remote(piece, piece, send, recv, device).start()

    def spread(k):
        piece = kv.at[:, rows(k, z)]

        @pl.when(k > 0)
        def _():
            wait_piece(piece, s1_recv.at[k])
        push(piece, ring_send.at[0], up_recv.at[k], up)
        push(piece, ring_send.at[1], dn_recv.at[k], dn)
        push(piece, sib_send.at[0], sib_recv.at[0], sib)

    def relay(k):
        low = kv.at[:, rows(k, z_dn)]
        high = kv.at[:, rows(k, z_up)]
        wait_piece(low, up_recv.at[k])

        @pl.when(lax.rem(k, 2) == 0)
        def _():
            push(low, ring_send.at[2], far_recv.at[k], up)
        push(low, sib_send.at[1], sib_recv.at[1], sib)
        wait_piece(high, dn_recv.at[k])

        @pl.when(lax.rem(k, 2) == 1)
        def _():
            push(high, ring_send.at[3], far_recv.at[k], dn)
        push(high, sib_send.at[2], sib_recv.at[2], sib)

    def last(k):
        piece = kv.at[:, rows(k, z_far)]
        wait_piece(piece, far_recv.at[k])
        push(piece, sib_send.at[3], sib_recv.at[3], sib)

    @pl.loop(0, 16 + LAG_FAR)
    def _(i):
        @pl.when(i < 16)
        def _():
            spread(i)

        @pl.when((i >= LAG) & (i < 16 + LAG))
        def _():
            relay(i - LAG)

        @pl.when(i >= LAG_FAR)
        def _():
            last(i - LAG_FAR)

    own[2].wait()
    wait_piece(qb.at[pl.ds(0, 15 * SHARE)], q_recv)
    span = kv.at[:, pl.ds(0, 64)]
    for i in range(4):
        wait_piece(span, sib_recv.at[i])

    @pl.loop(0, 16 // GANG)
    def _(g):
        lists, queries = [], []
        for i in range(GANG):
            px, py = peer(g * GANG + i)
            first = token_share(px, py, z, core) * 4
            for j in range(4):
                b = first + j
                lists.append([
                    lax.rem(b + NB - 1, NB), b, lax.rem(b + 1, NB), 0, 1,
                    rand[0, b], rand[1, b], rand[2, b],
                ])
                start = pl.multiple_of(g * GANG * SHARE + (i * 4 + j) * BLK, BLK)
                queries.append(qb[pl.ds(start, BLK), :])

        def listed(side, picks):
            return jnp.concatenate([kv[side, pick] for pick in picks], axis=0)

        scores = [
            lax.dot_general(q, listed(0, picks), (((1,), (1,)), ((), ())), preferred_element_type=jnp.float32)
            for q, picks in zip(queries, lists)
        ]
        peaks = [jnp.max(s, axis=-1, keepdims=True) for s in scores]
        lifted = [jnp.exp2((s - peak) * EXP_SCALE) for s, peak in zip(scores, peaks)]
        scales = [1.0 / jnp.sum(e, axis=-1, keepdims=True) for e in lifted]
        weights = [(e * scale).astype(jnp.bfloat16) for e, scale in zip(lifted, scales)]
        outs = [
            jnp.dot(w, listed(1, picks), preferred_element_type=jnp.float32).astype(jnp.bfloat16)
            for w, picks in zip(weights, lists)
        ]
        start = pl.multiple_of(g * GANG * SHARE, GANG * SHARE)
        ob[pl.ds(start, GANG * SHARE), :] = jnp.concatenate(outs, axis=0)
        for i in range(GANG):
            k = g * GANG + i
            px, py = peer(k)
            slot = pl.ds(pl.multiple_of(k * SHARE, SHARE), SHARE)

            @pl.when(k > 0)
            def _():
                remote(ob.at[slot], att.at[:, lanes(head)], ret_send, ret_recv, mesh_id(px, py, z, core)).start()

    keep = pltpu.make_async_copy(ob.at[pl.ds(0, SHARE)], att.at[:, lanes(head)], own_sem.at[0])
    keep.start()
    for copy in w_copies:
        copy.wait()
    keep.wait()
    fifteen = ob.at[pl.ds(0, 15 * SHARE)]
    wait_piece(fifteen, ret_recv)

    @pl.loop(0, D // TILE_N)
    def _(n):
        cols = pl.ds(pl.multiple_of(n * TILE_N, TILE_N), TILE_N)
        outv[:, cols] = jnp.dot(att[...], wv[:, cols], preferred_element_type=jnp.float32).astype(jnp.bfloat16)
        pltpu.make_async_copy(outv.at[:, cols], out.at[:, cols], out_sem).start()

    wait_piece(outv, out_sem)
    wait_piece(fifteen, ret_send)
    for i in range(3):
        wait_piece(fifteen, s1_send.at[i])
    for i in range(2):
        wait_piece(span, ring_send.at[i])
    half = kv.at[:, pl.ds(0, 32)]
    for i in range(2, 4):
        wait_piece(half, ring_send.at[i])
    for i in range(4):
        wait_piece(span, sib_send.at[i])


def shards(queries, keys, values, rand_blocks, out_weight):
    any_spec = pl.BlockSpec(memory_space=pl.ANY)
    dma = pltpu.SemaphoreType.DMA
    return pl.pallas_call(
        kernel,
        out_shape=jax.ShapeDtypeStruct((SHARE, D), jnp.bfloat16),
        in_specs=[pl.BlockSpec(memory_space=pltpu.SMEM)] + [any_spec] * 4,
        out_specs=any_spec,
        scratch_shapes=[
            pltpu.VMEM((2, NB, BLK, DH), jnp.bfloat16),
            pltpu.VMEM((16 * SHARE, DH), jnp.bfloat16),
            pltpu.VMEM((16 * SHARE, DH), jnp.bfloat16),
            pltpu.VMEM((SHARE, H * DH), jnp.bfloat16),
            pltpu.VMEM((H * DH, D), jnp.bfloat16),
            pltpu.VMEM((SHARE, D), jnp.bfloat16),
            dma((3,)), dma((3,)), dma((16,)), dma, dma((16,)), dma((16,)), dma((16,)),
            dma((4,)), dma((4,)), dma((4,)), dma, dma, dma((8,)), dma,
        ],
        compiler_params=pltpu.CompilerParams(
            collective_id=0, has_side_effects=True, vmem_limit_bytes=56 * 1024 * 1024),
    )(rand_blocks.T, queries, keys.reshape(4, BLK, H * DH), values.reshape(4, BLK, H * DH), out_weight)


def solution(mesh):
    return jax.shard_map(
        shards,
        mesh=mesh,
        in_specs=(
            P(("ctx", "ulys"), None),
            P(("ctx", "ulys"), None),
            P(("ctx", "ulys"), None),
            P(),
            P(),
        ),
        out_specs=P(("ctx", "ulys"), None),
        check_vma=False,
    )
```

```python
import functools

import jax
import jax.numpy as jnp
from jax import lax
from jax.experimental import pallas as pl
from jax.experimental.pallas import tpu as pltpu
from jax.sharding import PartitionSpec as P

H = 16
DH = 128
D = 4096
BLK = 64
NB = 512
TOKENS = 32768
SHARE = 256
MESH = pl.DeviceIdType.MESH
TILE_N = 512
LAG = 6
LAG_FAR = 12
WEIGH_AT = 28
FIRST_AT = 36
VMEM_MIB = 47
GANG = 2
EXP_SCALE = (DH ** -0.5) * 1.4426950408889634


def mesh_id(x, y, z, core):
    return ((lax.rem(z, 2) * 4 + y) * 2 + core, lax.div(z, 2) * 4 + x)


def token_share(x, y, z, core):
    ctx, ulys = mesh_id(x, y, z, core)
    return ctx * 8 + ulys


def kernel(rand, q_in, k_in, v_in, w_in, out,
           kb, vb0, vb1, qb, pb, va, vp, ob, att, wv, acc,
           own_sem, s1_send, k_recv, v_recv, q_recv, k_up, k_dn, k_far, v_up, v_dn, v_far,
           ring_send, sib_send, sib_recv, ret_send, ret_recv, w_sem, out_sem):
    ctx, ulys = lax.axis_index("ctx"), lax.axis_index("ulys")
    core = lax.rem(ctx, 2)
    y = lax.rem(lax.div(ctx, 2), 4)
    z = lax.div(ulys, 4) * 2 + lax.div(ctx, 8)
    x = lax.rem(ulys, 4)
    head = y * 4 + x
    z_up, z_dn, z_far = lax.rem(z + 1, 4), lax.rem(z + 3, 4), lax.rem(z + 2, 4)
    up, dn = mesh_id(x, y, z_up, core), mesh_id(x, y, z_dn, core)
    sib = mesh_id(x, y, z, 1 - core)
    vbs = (vb0, vb1)

    def peer(k):
        return lax.rem(x + lax.rem(k, 4), 4), lax.rem(y + lax.div(k, 4), 4)

    def back(k):
        return lax.rem(x + 4 - lax.rem(k, 4), 4), lax.rem(y + 4 - lax.div(k, 4), 4)

    def lanes(h):
        return pl.ds(pl.multiple_of(h * DH, DH), DH)

    def rows(k, zz):
        px, py = peer(k)
        return pl.ds(token_share(px, py, zz, core) * 4, 4)

    def rows_x(g, zz):
        return pl.ds(token_share(0, lax.rem(y + g, 4), zz, core) * 4, 16)

    def shares(k, count=1):
        return pl.ds(pl.multiple_of(k * SHARE, SHARE), count * SHARE)

    def packed(k, count=1):
        return pl.ds(pl.multiple_of(k * DH, DH), count * DH)

    my_rows = rows(0, z)
    own = [
        pltpu.make_async_copy(k_in.at[:, :, lanes(head)], kb.at[my_rows], own_sem.at[0]),
        pltpu.make_async_copy(v_in, va, own_sem.at[1]),
        pltpu.make_async_copy(q_in.at[:, lanes(head)], qb.at[shares(0)], own_sem.at[2]),
    ]
    for copy in own:
        copy.start()

    barrier = pltpu.get_barrier_semaphore()
    for device in (up, dn, sib):
        pl.semaphore_signal(barrier, inc=1, device_id=device, device_id_type=MESH)

    @pl.loop(1, 16)
    def _(k):
        px, py = back(k)
        pl.semaphore_signal(barrier, inc=1, device_id=mesh_id(px, py, z, core), device_id_type=MESH)

    pl.semaphore_wait(barrier, 18)

    def push(src, dst, send, recv, device):
        pltpu.make_async_remote_copy(
            src_ref=src, dst_ref=dst, send_sem=send, recv_sem=recv,
            device_id=device, device_id_type=MESH).start()

    def arrived(piece, sem):
        pltpu.make_async_copy(piece, piece, sem).wait()

    def send_on(side, piece, via, sem, device):
        push(piece, piece, ring_send.at[side, via], sem, device)

    def share_on(side, piece, plane):
        push(piece, piece, sib_send.at[side, plane], sib_recv.at[side, plane], sib)

    def relay(side, low, high, from_low, from_high, to_far, k):
        arrived(low, from_low)

        @pl.when(lax.rem(k, 2) == 0)
        def _():
            send_on(side, low, 2, to_far, up)
        share_on(side, low, 1)
        arrived(high, from_high)

        @pl.when(lax.rem(k, 2) == 1)
        def _():
            send_on(side, high, 3, to_far, dn)
        share_on(side, high, 2)

    def spread_k(k):
        piece = kb.at[rows(k, z)]
        send_on(0, piece, 0, k_up.at[k], up)
        send_on(0, piece, 1, k_dn.at[k], dn)
        share_on(0, piece, 0)

    def relay_k(k):
        relay(0, kb.at[rows(k, z_dn)], kb.at[rows(k, z_up)], k_up.at[k], k_dn.at[k], k_far.at[k], k)

    def last_k(k):
        piece = kb.at[rows(k, z_far)]
        arrived(piece, k_far.at[k])
        share_on(0, piece, 3)

    def spread_v(h, g):
        piece = vbs[h].at[rows_x(g, z)]
        arrived(piece, v_recv.at[h, g])
        send_on(1 + h, piece, 0, v_up.at[h, g], up)
        send_on(1 + h, piece, 1, v_dn.at[h, g], dn)
        share_on(1 + h, piece, 0)

    def relay_v(h, g):
        relay(1 + h, vbs[h].at[rows_x(g, z_dn)], vbs[h].at[rows_x(g, z_up)],
              v_up.at[h, g], v_dn.at[h, g], v_far.at[h, g], g)

    def last_v(h, g):
        piece = vbs[h].at[rows_x(g, z_far)]
        arrived(piece, v_far.at[h, g])
        share_on(1 + h, piece, 3)

    own[0].wait()
    spread_k(0)

    @pl.loop(1, 16)
    def _(k):
        px, py = back(k)
        push(k_in.at[:, :, lanes(py * 4 + px)], kb.at[my_rows], s1_send.at[0], k_recv.at[k], mesh_id(px, py, z, core))

    @pl.loop(1, 16)
    def _(k):
        px, py = back(k)
        push(q_in.at[:, lanes(py * 4 + px)], qb.at[shares(k)], s1_send.at[1], q_recv, mesh_id(px, py, z, core))

    own[1].wait()
    lane = lax.broadcasted_iota(jnp.int32, (1, DH), 1)
    low_half = lane < DH // 2

    def swap(a):
        return pltpu.roll(a, DH // 2, axis=1)

    @pl.loop(0, 16)
    def _(h):
        for blk in range(4):
            top = va[blk * BLK:blk * BLK + 32, lanes(h)].astype(jnp.float32)
            bottom = va[blk * BLK + 32:blk * BLK + 64, lanes(h)].astype(jnp.float32)
            vp[0, h, blk] = jnp.where(low_half, top, swap(bottom)).astype(jnp.bfloat16)
            vp[1, h, blk] = jnp.where(low_half, swap(top), bottom).astype(jnp.bfloat16)

    for h in range(2):
        pltpu.make_async_copy(vp.at[h, head], vbs[h].at[my_rows], v_recv.at[h, 0]).start()

        @pl.loop(1, 16)
        def _(k):
            px, py = back(k)
            push(vp.at[h, py * 4 + px], vbs[h].at[my_rows], s1_send.at[2 + h], v_recv.at[h, lax.div(k, 4)],
                 mesh_id(px, py, z, core))

    for h in range(2):
        @pl.loop(0, 16)
        def _(k):
            px, py = back(k)
            pltpu.make_async_copy(
                w_in.at[pl.ds(pl.multiple_of((py * 4 + px) * DH + h * 64, 64), 64)],
                wv.at[h, pl.ds(pl.multiple_of(k * 64, 64), 64)], w_sem.at[h]).start()
    own[2].wait()

    def blocks_of(g):
        found = []
        for i in range(GANG):
            px, py = peer(g * GANG + i)
            first = token_share(px, py, z, core) * 4
            for j in range(4):
                b = first + j
                found.append([
                    lax.rem(b + NB - 1, NB), b, lax.rem(b + 1, NB), 0, 1,
                    rand[0, b], rand[1, b], rand[2, b],
                ])
        return found

    def gang_rows(g, n):
        return pl.ds(pl.multiple_of(g * GANG * SHARE + n * BLK, BLK), BLK)

    def listed_keys(picks):
        blocks = [kb[pick] for pick in picks]
        return jnp.concatenate([b[0:32] for b in blocks] + [b[32:64] for b in blocks], axis=0)

    def weigh(g):
        scores = [
            lax.dot_general(qb[gang_rows(g, n), :], listed_keys(picks), (((1,), (1,)), ((), ())),
                            preferred_element_type=jnp.float32)
            for n, picks in enumerate(blocks_of(g))
        ]
        peaks = [jnp.max(s, axis=-1, keepdims=True) for s in scores]
        lifted = [jnp.exp2((s - peak) * EXP_SCALE) for s, peak in zip(scores, peaks)]
        scales = [1.0 / jnp.sum(e, axis=-1, keepdims=True) for e in lifted]
        for n, (e, scale) in enumerate(zip(lifted, scales)):
            pb[gang_rows(g, n), :] = (e * scale).astype(jnp.bfloat16)

    def attend(h, g):
        sums = []
        for n, picks in enumerate(blocks_of(g)):
            w = pb[gang_rows(g, n), :]
            w = jnp.concatenate([w[:, 0:256], w[:, 256:512]], axis=0)
            listed = jnp.concatenate([vbs[h][pick] for pick in picks], axis=0)
            sums.append(jnp.dot(w, listed, preferred_element_type=jnp.float32))
        outs = []
        for even, odd in zip(sums[0::2], sums[1::2]):
            outs.append(jnp.where(low_half, even[0:64] + swap(even[64:128]), swap(odd[0:64]) + odd[64:128]))
        ob[h, packed(g * GANG, GANG), :] = jnp.concatenate(outs, axis=0).astype(jnp.bfloat16)
        for i in range(GANG):
            k = g * GANG + i
            px, py = peer(k)

            @pl.when(k > 0)
            def _():
                push(ob.at[h, packed(k)], att.at[h, :, lanes(k)], ret_send.at[h], ret_recv.at[h], mesh_id(px, py, z, core))

            @pl.when(k == 0)
            def _():
                pltpu.make_async_copy(ob.at[h, packed(0)], att.at[h, :, pl.ds(0, DH)], ret_recv.at[h]).start()

    span = pl.ds(0, 64)
    half = pl.ds(0, 32)

    def at(i, begin, end):
        return (i >= begin) & (i < end)

    def at_even(i, begin):
        return (i >= begin) & (i < begin + 8) & (lax.rem(i - begin, 2) == 0)

    @pl.loop(1, 32 + LAG_FAR)
    def _(i):
        @pl.when(i < 16)
        def _():
            arrived(kb.at[rows(i, z)], k_recv.at[i])
            spread_k(i)

        for h in range(2):
            @pl.when(at_even(i, 16 + 8 * h))
            def _():
                spread_v(h, lax.div(i - 16 - 8 * h, 2))

        @pl.when(at(i, LAG, 16 + LAG))
        def _():
            relay_k(i - LAG)

        for h in range(2):
            @pl.when(at_even(i, 16 + 8 * h + LAG))
            def _():
                relay_v(h, lax.div(i - 16 - 8 * h - LAG, 2))

        @pl.when(at(i, LAG_FAR, 16 + LAG_FAR))
        def _():
            last_k(i - LAG_FAR)

        for h in range(2):
            @pl.when(at_even(i, 16 + 8 * h + LAG_FAR))
            def _():
                last_v(h, lax.div(i - 16 - 8 * h - LAG_FAR, 2))

        @pl.when(i == WEIGH_AT - 1)
        def _():
            arrived(qb.at[shares(0, 15)], q_recv)
            for plane in range(4):
                arrived(kb.at[span], sib_recv.at[0, plane])

        @pl.when(at(i, WEIGH_AT, WEIGH_AT + 16 // GANG))
        def _():
            weigh(i - WEIGH_AT)

        @pl.when(i == FIRST_AT - 1)
        def _():
            for plane in range(4):
                arrived(vb0.at[span], sib_recv.at[1, plane])

        @pl.when(at(i, FIRST_AT, FIRST_AT + 16 // GANG))
        def _():
            attend(0, i - FIRST_AT)

    for plane in range(4):
        arrived(vb1.at[span], sib_recv.at[2, plane])

    @pl.loop(0, 16 // GANG)
    def _(g):
        attend(1, g)

    def unpack(h):
        for pair in range(8):
            a = att[h, :, 2 * pair * DH:(2 * pair + 1) * DH].astype(jnp.float32)
            b = att[h, :, (2 * pair + 1) * DH:(2 * pair + 2) * DH].astype(jnp.float32)
            cols = slice(h * 1024 + pair * DH, h * 1024 + (pair + 1) * DH)
            va[0:128, cols] = jnp.where(low_half, a, swap(b)).astype(jnp.bfloat16)
            va[128:256, cols] = jnp.where(low_half, swap(a), b).astype(jnp.bfloat16)

    def tile(n):
        return pl.ds(pl.multiple_of(n * TILE_N, TILE_N), TILE_N)

    arrived(wv.at[0], w_sem.at[0])
    arrived(ob.at[0], ret_recv.at[0])
    unpack(0)

    @pl.loop(0, D // TILE_N)
    def _(n):
        acc[:, tile(n)] = jnp.dot(va[:, 0:1024], wv[0, :, tile(n)], preferred_element_type=jnp.float32)

    arrived(wv.at[1], w_sem.at[1])
    arrived(ob.at[1], ret_recv.at[1])
    unpack(1)

    @pl.loop(0, D // TILE_N)
    def _(n):
        total = acc[:, tile(n)] + jnp.dot(va[:, 1024:2048], wv[1, :, tile(n)], preferred_element_type=jnp.float32)
        total = total.astype(jnp.bfloat16)
        done = jnp.concatenate([total[0:64], total[128:192], total[64:128], total[192:256]], axis=0)
        pb[shares(n), :] = done
        pltpu.make_async_copy(pb.at[shares(n)], out.at[:, tile(n)], out_sem).start()

    for i in range(2):
        arrived(ob.at[0, packed(0, 15)], ret_send.at[i])
        arrived(qb.at[shares(0, 15)], s1_send.at[i])
        arrived(ob.at[0, packed(0, 15)], s1_send.at[2 + i])
    for side, buf in enumerate((kb, vb0, vb1)):
        for i in range(2):
            arrived(buf.at[span], ring_send.at[side, i])
        for i in range(2, 4):
            arrived(buf.at[half], ring_send.at[side, i])
        for i in range(4):
            arrived(buf.at[span], sib_send.at[side, i])
    arrived(pb.at[shares(0, D // TILE_N)], out_sem)


def shards(queries, keys, values, rand_blocks, out_weight):
    any_spec = pl.BlockSpec(memory_space=pl.ANY)
    dma = pltpu.SemaphoreType.DMA
    return pl.pallas_call(
        kernel,
        out_shape=jax.ShapeDtypeStruct((SHARE, D), jnp.bfloat16),
        in_specs=[pl.BlockSpec(memory_space=pltpu.SMEM)] + [any_spec] * 4,
        out_specs=any_spec,
        scratch_shapes=[
            pltpu.VMEM((NB, BLK, DH), jnp.bfloat16),
            pltpu.VMEM((NB, BLK // 2, DH), jnp.bfloat16),
            pltpu.VMEM((NB, BLK // 2, DH), jnp.bfloat16),
            pltpu.VMEM((16 * SHARE, DH), jnp.bfloat16),
            pltpu.VMEM((16 * SHARE, 8 * BLK), jnp.bfloat16),
            pltpu.VMEM((SHARE, H * DH), jnp.bfloat16),
            pltpu.VMEM((2, H, 4, BLK // 2, DH), jnp.bfloat16),
            pltpu.VMEM((2, 16 * SHARE // 2, DH), jnp.bfloat16),
            pltpu.VMEM((2, SHARE // 2, H * DH), jnp.bfloat16),
            pltpu.VMEM((2, H * DH // 2, D), jnp.bfloat16),
            pltpu.VMEM((SHARE, D), jnp.float32),
            dma((3,)), dma((4,)), dma((16,)), dma((2, 4)), dma,
            dma((16,)), dma((16,)), dma((16,)), dma((2, 4)), dma((2, 4)), dma((2, 4)),
            dma((3, 4)), dma((3, 4)), dma((3, 4)), dma((2,)), dma((2,)), dma((2,)), dma,
        ],
        compiler_params=pltpu.CompilerParams(
            collective_id=0, has_side_effects=True, vmem_limit_bytes=VMEM_MIB * 1024 * 1024),
    )(rand_blocks.T, queries, keys.reshape(4, BLK, H * DH), values, out_weight)


def solution(mesh):
    return jax.shard_map(
        shards,
        mesh=mesh,
        in_specs=(
            P(("ctx", "ulys"), None),
            P(("ctx", "ulys"), None),
            P(("ctx", "ulys"), None),
            P(),
            P(),
        ),
        out_specs=P(("ctx", "ulys"), None),
        check_vma=False,
    )
```

```python
import functools

import jax
import jax.numpy as jnp
from jax import lax
from jax.experimental import pallas as pl
from jax.experimental.pallas import tpu as pltpu
from jax.sharding import PartitionSpec as P

H = 16
DH = 128
D = 4096
BLK = 64
NB = 512
TOKENS = 32768
SHARE = 256
MESH = pl.DeviceIdType.MESH
TILE_N = 512
LAG = 6
LAG_FAR = 12
V_AT = (16, 26)
V_LAG = 4
V_FAR = 8
Q_AT = 4
PACK_AT = 6
W_AT = 10
WEIGH_AT = 28
FIRST_AT = 32
STOP = 42
VMEM_MIB = 47
GANG = 2
EXP_SCALE = (DH ** -0.5) * 1.4426950408889634


def mesh_id(x, y, z, core):
    return ((lax.rem(z, 2) * 4 + y) * 2 + core, lax.div(z, 2) * 4 + x)


def token_share(x, y, z, core):
    ctx, ulys = mesh_id(x, y, z, core)
    return ctx * 8 + ulys


def kernel(rand, q_in, k_in, v_in, w_in, out,
           kb, vb0, vb1, qb, pb, va, vp, ob, att, wv, acc,
           own_sem, s1_send, k_recv, v_recv, q_recv, k_up, k_dn, k_far, v_up, v_dn, v_far,
           ring_send, sib_send, sib_recv, ret_send, ret_recv, w_sem, out_sem):
    ctx, ulys = lax.axis_index("ctx"), lax.axis_index("ulys")
    core = lax.rem(ctx, 2)
    y = lax.rem(lax.div(ctx, 2), 4)
    z = lax.div(ulys, 4) * 2 + lax.div(ctx, 8)
    x = lax.rem(ulys, 4)
    head = y * 4 + x
    z_up, z_dn, z_far = lax.rem(z + 1, 4), lax.rem(z + 3, 4), lax.rem(z + 2, 4)
    up, dn = mesh_id(x, y, z_up, core), mesh_id(x, y, z_dn, core)
    sib = mesh_id(x, y, z, 1 - core)
    vbs = (vb0, vb1)

    def peer(k):
        return lax.rem(x + lax.rem(k, 4), 4), lax.rem(y + lax.div(k, 4), 4)

    def back(k):
        return lax.rem(x + 4 - lax.rem(k, 4), 4), lax.rem(y + 4 - lax.div(k, 4), 4)

    def lanes(h):
        return pl.ds(pl.multiple_of(h * DH, DH), DH)

    def rows(k, zz):
        px, py = peer(k)
        return pl.ds(token_share(px, py, zz, core) * 4, 4)

    def rows_x(g, zz):
        return pl.ds(token_share(0, lax.rem(y + g, 4), zz, core) * 4, 16)

    def shares(k, count=1):
        return pl.ds(pl.multiple_of(k * SHARE, SHARE), count * SHARE)

    def packed(k, count=1):
        return pl.ds(pl.multiple_of(k * DH, DH), count * DH)

    my_rows = rows(0, z)
    own = [
        pltpu.make_async_copy(k_in.at[:, :, lanes(head)], kb.at[my_rows], own_sem.at[0]),
        pltpu.make_async_copy(v_in, va, own_sem.at[1]),
        pltpu.make_async_copy(q_in.at[:, lanes(head)], qb.at[shares(0)], own_sem.at[2]),
    ]
    for copy in own:
        copy.start()

    barrier = pltpu.get_barrier_semaphore()
    for device in (up, dn, sib):
        pl.semaphore_signal(barrier, inc=1, device_id=device, device_id_type=MESH)

    @pl.loop(1, 16)
    def _(k):
        px, py = back(k)
        pl.semaphore_signal(barrier, inc=1, device_id=mesh_id(px, py, z, core), device_id_type=MESH)

    pl.semaphore_wait(barrier, 18)

    def push(src, dst, send, recv, device):
        pltpu.make_async_remote_copy(
            src_ref=src, dst_ref=dst, send_sem=send, recv_sem=recv,
            device_id=device, device_id_type=MESH).start()

    def arrived(piece, sem):
        pltpu.make_async_copy(piece, piece, sem).wait()

    def send_on(side, piece, via, sem, device):
        push(piece, piece, ring_send.at[side, via], sem, device)

    def share_on(side, piece, plane):
        push(piece, piece, sib_send.at[side, plane], sib_recv.at[side, plane], sib)

    def relay(side, low, high, from_low, from_high, to_far, k):
        arrived(low, from_low)

        @pl.when(lax.rem(k, 2) == 0)
        def _():
            send_on(side, low, 2, to_far, up)
        share_on(side, low, 1)
        arrived(high, from_high)

        @pl.when(lax.rem(k, 2) == 1)
        def _():
            send_on(side, high, 3, to_far, dn)
        share_on(side, high, 2)

    def spread_k(k):
        piece = kb.at[rows(k, z)]
        send_on(0, piece, 0, k_up.at[k], up)
        send_on(0, piece, 1, k_dn.at[k], dn)
        share_on(0, piece, 0)

    def relay_k(k):
        relay(0, kb.at[rows(k, z_dn)], kb.at[rows(k, z_up)], k_up.at[k], k_dn.at[k], k_far.at[k], k)

    def last_k(k):
        piece = kb.at[rows(k, z_far)]
        arrived(piece, k_far.at[k])
        share_on(0, piece, 3)

    def spread_v(h, g):
        piece = vbs[h].at[rows_x(g, z)]
        arrived(piece, v_recv.at[h, g])
        send_on(1 + h, piece, 0, v_up.at[h, g], up)
        send_on(1 + h, piece, 1, v_dn.at[h, g], dn)
        share_on(1 + h, piece, 0)

    def relay_v(h, g):
        relay(1 + h, vbs[h].at[rows_x(g, z_dn)], vbs[h].at[rows_x(g, z_up)],
              v_up.at[h, g], v_dn.at[h, g], v_far.at[h, g], g)

    def last_v(h, g):
        piece = vbs[h].at[rows_x(g, z_far)]
        arrived(piece, v_far.at[h, g])
        share_on(1 + h, piece, 3)

    own[0].wait()
    spread_k(0)

    @pl.loop(1, 16)
    def _(k):
        px, py = back(k)
        push(k_in.at[:, :, lanes(py * 4 + px)], kb.at[my_rows], s1_send.at[0], k_recv.at[k], mesh_id(px, py, z, core))

    def send_queries():
        @pl.loop(1, 16)
        def _(k):
            px, py = back(k)
            push(q_in.at[:, lanes(py * 4 + px)], qb.at[shares(k)], s1_send.at[1], q_recv, mesh_id(px, py, z, core))

    lane = lax.broadcasted_iota(jnp.int32, (1, DH), 1)
    low_half = lane < DH // 2

    def swap(a):
        return pltpu.roll(a, DH // 2, axis=1)

    def send_values():
        own[1].wait()

        @pl.loop(0, 16)
        def _(h):
            for blk in range(4):
                top = va[blk * BLK:blk * BLK + 32, lanes(h)].astype(jnp.float32)
                bottom = va[blk * BLK + 32:blk * BLK + 64, lanes(h)].astype(jnp.float32)
                vp[0, h, blk] = jnp.where(low_half, top, swap(bottom)).astype(jnp.bfloat16)
                vp[1, h, blk] = jnp.where(low_half, swap(top), bottom).astype(jnp.bfloat16)

        for h in range(2):
            pltpu.make_async_copy(vp.at[h, head], vbs[h].at[my_rows], v_recv.at[h, 0]).start()

            @pl.loop(1, 16)
            def _(k):
                px, py = back(k)
                push(vp.at[h, py * 4 + px], vbs[h].at[my_rows], s1_send.at[2 + h], v_recv.at[h, lax.div(k, 4)],
                     mesh_id(px, py, z, core))

    def load_weight():
        for h in range(2):
            @pl.loop(0, 16)
            def _(k):
                px, py = back(k)
                pltpu.make_async_copy(
                    w_in.at[pl.ds(pl.multiple_of((py * 4 + px) * DH + h * 64, 64), 64)],
                    wv.at[h, pl.ds(pl.multiple_of(k * 64, 64), 64)], w_sem.at[h]).start()

    def blocks_of(g):
        found = []
        for i in range(GANG):
            px, py = peer(g * GANG + i)
            first = token_share(px, py, z, core) * 4
            for j in range(4):
                b = first + j
                found.append([
                    lax.rem(b + NB - 1, NB), b, lax.rem(b + 1, NB), 0, 1,
                    rand[0, b], rand[1, b], rand[2, b],
                ])
        return found

    def gang_rows(g, n):
        return pl.ds(pl.multiple_of(g * GANG * SHARE + n * BLK, BLK), BLK)

    def listed_keys(picks):
        blocks = [kb[pick] for pick in picks]
        return jnp.concatenate([b[0:32] for b in blocks] + [b[32:64] for b in blocks], axis=0)

    def weigh(g):
        scores = [
            lax.dot_general(qb[gang_rows(g, n), :], listed_keys(picks), (((1,), (1,)), ((), ())),
                            preferred_element_type=jnp.float32)
            for n, picks in enumerate(blocks_of(g))
        ]
        peaks = [jnp.max(s, axis=-1, keepdims=True) for s in scores]
        lifted = [jnp.exp2((s - peak) * EXP_SCALE) for s, peak in zip(scores, peaks)]
        scales = [1.0 / jnp.sum(e, axis=-1, keepdims=True) for e in lifted]
        for n, (e, scale) in enumerate(zip(lifted, scales)):
            pb[gang_rows(g, n), :] = (e * scale).astype(jnp.bfloat16)

    def attend(h, g):
        sums = []
        for n, picks in enumerate(blocks_of(g)):
            w = pb[gang_rows(g, n), :]
            w = jnp.concatenate([w[:, 0:256], w[:, 256:512]], axis=0)
            listed = jnp.concatenate([vbs[h][pick] for pick in picks], axis=0)
            sums.append(jnp.dot(w, listed, preferred_element_type=jnp.float32))
        outs = []
        for even, odd in zip(sums[0::2], sums[1::2]):
            outs.append(jnp.where(low_half, even[0:64] + swap(even[64:128]), swap(odd[0:64]) + odd[64:128]))
        ob[h, packed(g * GANG, GANG), :] = jnp.concatenate(outs, axis=0).astype(jnp.bfloat16)
        for i in range(GANG):
            k = g * GANG + i
            px, py = peer(k)

            @pl.when(k > 0)
            def _():
                push(ob.at[h, packed(k)], att.at[h, :, lanes(k)], ret_send.at[h], ret_recv.at[h], mesh_id(px, py, z, core))

            @pl.when(k == 0)
            def _():
                pltpu.make_async_copy(ob.at[h, packed(0)], att.at[h, :, pl.ds(0, DH)], ret_recv.at[h]).start()

    span = pl.ds(0, 64)
    half = pl.ds(0, 32)

    def at(i, begin, end):
        return (i >= begin) & (i < end)

    def at_even(i, begin):
        return (i >= begin) & (i < begin + 8) & (lax.rem(i - begin, 2) == 0)

    @pl.loop(1, STOP)
    def _(i):
        @pl.when(i < 16)
        def _():
            arrived(kb.at[rows(i, z)], k_recv.at[i])
            spread_k(i)

        @pl.when(i == Q_AT)
        def _():
            send_queries()

        @pl.when(i == PACK_AT)
        def _():
            send_values()

        @pl.when(i == W_AT)
        def _():
            load_weight()

        for h in range(2):
            @pl.when(at_even(i, V_AT[h]))
            def _():
                spread_v(h, lax.div(i - V_AT[h], 2))

        @pl.when(at(i, LAG, 16 + LAG))
        def _():
            relay_k(i - LAG)

        for h in range(2):
            @pl.when(at_even(i, V_AT[h] + V_LAG))
            def _():
                relay_v(h, lax.div(i - V_AT[h] - V_LAG, 2))

        @pl.when(at(i, LAG_FAR, 16 + LAG_FAR))
        def _():
            last_k(i - LAG_FAR)

        for h in range(2):
            @pl.when(at_even(i, V_AT[h] + V_FAR))
            def _():
                last_v(h, lax.div(i - V_AT[h] - V_FAR, 2))

        @pl.when(i == WEIGH_AT - 1)
        def _():
            own[2].wait()
            arrived(qb.at[shares(0, 15)], q_recv)
            for plane in range(4):
                arrived(kb.at[span], sib_recv.at[0, plane])

        @pl.when(at(i, WEIGH_AT, WEIGH_AT + 16 // GANG))
        def _():
            weigh(i - WEIGH_AT)

        @pl.when(i == FIRST_AT - 1)
        def _():
            for plane in range(4):
                arrived(vb0.at[span], sib_recv.at[1, plane])

        @pl.when(at(i, FIRST_AT, FIRST_AT + 16 // GANG))
        def _():
            attend(0, i - FIRST_AT)

    for plane in range(4):
        arrived(vb1.at[span], sib_recv.at[2, plane])

    @pl.loop(0, 16 // GANG)
    def _(g):
        attend(1, g)

    def unpack(h):
        for pair in range(8):
            a = att[h, :, 2 * pair * DH:(2 * pair + 1) * DH].astype(jnp.float32)
            b = att[h, :, (2 * pair + 1) * DH:(2 * pair + 2) * DH].astype(jnp.float32)
            cols = slice(h * 1024 + pair * DH, h * 1024 + (pair + 1) * DH)
            va[0:128, cols] = jnp.where(low_half, a, swap(b)).astype(jnp.bfloat16)
            va[128:256, cols] = jnp.where(low_half, swap(a), b).astype(jnp.bfloat16)

    def tile(n):
        return pl.ds(pl.multiple_of(n * TILE_N, TILE_N), TILE_N)

    arrived(wv.at[0], w_sem.at[0])
    arrived(ob.at[0], ret_recv.at[0])
    unpack(0)

    @pl.loop(0, D // TILE_N)
    def _(n):
        acc[:, tile(n)] = jnp.dot(va[:, 0:1024], wv[0, :, tile(n)], preferred_element_type=jnp.float32)

    arrived(wv.at[1], w_sem.at[1])
    arrived(ob.at[1], ret_recv.at[1])
    unpack(1)

    @pl.loop(0, D // TILE_N)
    def _(n):
        total = acc[:, tile(n)] + jnp.dot(va[:, 1024:2048], wv[1, :, tile(n)], preferred_element_type=jnp.float32)
        total = total.astype(jnp.bfloat16)
        done = jnp.concatenate([total[0:64], total[128:192], total[64:128], total[192:256]], axis=0)
        pb[shares(n), :] = done
        pltpu.make_async_copy(pb.at[shares(n)], out.at[:, tile(n)], out_sem).start()

    for i in range(2):
        arrived(ob.at[0, packed(0, 15)], ret_send.at[i])
        arrived(qb.at[shares(0, 15)], s1_send.at[i])
        arrived(ob.at[0, packed(0, 15)], s1_send.at[2 + i])
    for side, buf in enumerate((kb, vb0, vb1)):
        for i in range(2):
            arrived(buf.at[span], ring_send.at[side, i])
        for i in range(2, 4):
            arrived(buf.at[half], ring_send.at[side, i])
        for i in range(4):
            arrived(buf.at[span], sib_send.at[side, i])
    arrived(pb.at[shares(0, D // TILE_N)], out_sem)


def shards(queries, keys, values, rand_blocks, out_weight):
    any_spec = pl.BlockSpec(memory_space=pl.ANY)
    hbm = pl.BlockSpec(memory_space=pltpu.HBM)
    dma = pltpu.SemaphoreType.DMA
    return pl.pallas_call(
        kernel,
        out_shape=jax.ShapeDtypeStruct((SHARE, D), jnp.bfloat16),
        in_specs=[pl.BlockSpec(memory_space=pltpu.SMEM)] + [hbm] * 4,
        out_specs=any_spec,
        scratch_shapes=[
            pltpu.VMEM((NB, BLK, DH), jnp.bfloat16),
            pltpu.VMEM((NB, BLK // 2, DH), jnp.bfloat16),
            pltpu.VMEM((NB, BLK // 2, DH), jnp.bfloat16),
            pltpu.VMEM((16 * SHARE, DH), jnp.bfloat16),
            pltpu.VMEM((16 * SHARE, 8 * BLK), jnp.bfloat16),
            pltpu.VMEM((SHARE, H * DH), jnp.bfloat16),
            pltpu.VMEM((2, H, 4, BLK // 2, DH), jnp.bfloat16),
            pltpu.VMEM((2, 16 * SHARE // 2, DH), jnp.bfloat16),
            pltpu.VMEM((2, SHARE // 2, H * DH), jnp.bfloat16),
            pltpu.VMEM((2, H * DH // 2, D), jnp.bfloat16),
            pltpu.VMEM((SHARE, D), jnp.float32),
            dma((3,)), dma((4,)), dma((16,)), dma((2, 4)), dma,
            dma((16,)), dma((16,)), dma((16,)), dma((2, 4)), dma((2, 4)), dma((2, 4)),
            dma((3, 4)), dma((3, 4)), dma((3, 4)), dma((2,)), dma((2,)), dma((2,)), dma,
        ],
        compiler_params=pltpu.CompilerParams(
            collective_id=0, has_side_effects=True, vmem_limit_bytes=VMEM_MIB * 1024 * 1024),
    )(rand_blocks.T, *[pltpu.with_memory_space_constraint(a, pltpu.HBM) for a in (queries, keys.reshape(4, BLK, H * DH), values, out_weight)])


def solution(mesh):
    return jax.shard_map(
        shards,
        mesh=mesh,
        in_specs=(
            P(("ctx", "ulys"), None),
            P(("ctx", "ulys"), None),
            P(("ctx", "ulys"), None),
            P(),
            P(),
        ),
        out_specs=P(("ctx", "ulys"), None),
        check_vma=False,
    )
```

```python
import functools

import jax
import jax.numpy as jnp
from jax import lax
from jax.experimental import pallas as pl
from jax.experimental.pallas import tpu as pltpu
from jax.sharding import PartitionSpec as P

H = 16
DH = 128
D = 4096
BLK = 64
NB = 512
TOKENS = 32768
SHARE = 256
MESH = pl.DeviceIdType.MESH
TILE_N = 512
LAG = 6
LAG_FAR = 12
V_AT = (16, 26)
V_LAG = 4
V_FAR = 8
Q_AT = 4
PACK_AT = 6
W_AT = 10
WEIGH_AT = 28
FIRST_AT = 32
STOP = 42
VMEM_MIB = 47
GANG = 2
EXP_SCALE = (DH ** -0.5) * 1.4426950408889634


def mesh_id(x, y, z, core):
    return ((lax.rem(z, 2) * 4 + y) * 2 + core, lax.div(z, 2) * 4 + x)


def token_share(x, y, z, core):
    ctx, ulys = mesh_id(x, y, z, core)
    return ctx * 8 + ulys


def kernel(rand, q_in, k_in, v_in, w_in, out,
           kb, vb0, vb1, qb, pb, va, vp, ob, att, wv, acc,
           own_sem, s1_send, k_recv, v_recv, q_recv, k_up, k_dn, k_far, v_up, v_dn, v_far,
           ring_send, sib_send, sib_recv, ret_send, ret_recv, w_sem, out_sem, row_in):
    ctx, ulys = lax.axis_index("ctx"), lax.axis_index("ulys")
    core = lax.rem(ctx, 2)
    y = lax.rem(lax.div(ctx, 2), 4)
    z = lax.div(ulys, 4) * 2 + lax.div(ctx, 8)
    x = lax.rem(ulys, 4)
    head = y * 4 + x
    z_up, z_dn, z_far = lax.rem(z + 1, 4), lax.rem(z + 3, 4), lax.rem(z + 2, 4)
    up, dn = mesh_id(x, y, z_up, core), mesh_id(x, y, z_dn, core)
    sib = mesh_id(x, y, z, 1 - core)
    vbs = (vb0, vb1)

    def peer(k):
        return lax.rem(x + lax.rem(k, 4), 4), lax.rem(y + lax.div(k, 4), 4)

    def back(k):
        return lax.rem(x + 4 - lax.rem(k, 4), 4), lax.rem(y + 4 - lax.div(k, 4), 4)

    def lanes(h):
        return pl.ds(pl.multiple_of(h * DH, DH), DH)

    def rows(k, zz):
        px, py = peer(k)
        return pl.ds(token_share(px, py, zz, core) * 4, 4)

    def rows_x(g, zz):
        return pl.ds(token_share(lax.rem(g, 2) * 2, lax.rem(y + lax.div(g, 2), 4), zz, core) * 4, 8)

    def shares(k, count=1):
        return pl.ds(pl.multiple_of(k * SHARE, SHARE), count * SHARE)

    def packed(k, count=1):
        return pl.ds(pl.multiple_of(k * DH, DH), count * DH)

    my_rows = rows(0, z)
    own = [
        pltpu.make_async_copy(k_in.at[:, :, lanes(head)], kb.at[my_rows], own_sem.at[0]),
        pltpu.make_async_copy(v_in, va, own_sem.at[1]),
        pltpu.make_async_copy(q_in.at[:, lanes(head)], qb.at[shares(0)], own_sem.at[2]),
    ]
    for copy in own:
        copy.start()

    barrier = pltpu.get_barrier_semaphore()
    for device in (up, dn, sib):
        pl.semaphore_signal(barrier, inc=1, device_id=device, device_id_type=MESH)
    for k in (1, 2, 3, 4, 8, 12):
        px, py = back(k)
        pl.semaphore_signal(barrier, inc=1, device_id=mesh_id(px, py, z, core), device_id_type=MESH)
    pl.semaphore_wait(barrier, 9)
    for k in (4, 8, 12):
        px, py = back(k)
        pl.semaphore_signal(row_in, inc=1, device_id=mesh_id(px, py, z, core), device_id_type=MESH)

    def push(src, dst, send, recv, device):
        pltpu.make_async_remote_copy(
            src_ref=src, dst_ref=dst, send_sem=send, recv_sem=recv,
            device_id=device, device_id_type=MESH).start()

    def arrived(piece, sem):
        pltpu.make_async_copy(piece, piece, sem).wait()

    def send_on(side, piece, via, sem, device):
        push(piece, piece, ring_send.at[side, via], sem, device)

    def share_on(side, piece, plane):
        push(piece, piece, sib_send.at[side, plane], sib_recv.at[side, plane], sib)

    def relay(side, low, high, from_low, from_high, to_far, k):
        arrived(low, from_low)

        @pl.when(lax.rem(k, 2) == 0)
        def _():
            send_on(side, low, 2, to_far, up)
        share_on(side, low, 1)
        arrived(high, from_high)

        @pl.when(lax.rem(k, 2) == 1)
        def _():
            send_on(side, high, 3, to_far, dn)
        share_on(side, high, 2)

    def spread_k(k):
        piece = kb.at[rows(k, z)]
        send_on(0, piece, 0, k_up.at[k], up)
        send_on(0, piece, 1, k_dn.at[k], dn)
        share_on(0, piece, 0)

    def relay_k(k):
        relay(0, kb.at[rows(k, z_dn)], kb.at[rows(k, z_up)], k_up.at[k], k_dn.at[k], k_far.at[k], k)

    def last_k(k):
        piece = kb.at[rows(k, z_far)]
        arrived(piece, k_far.at[k])
        share_on(0, piece, 3)

    def spread_v(h, g):
        piece = vbs[h].at[rows_x(g, z)]
        arrived(piece, v_recv.at[h, g])
        send_on(1 + h, piece, 0, v_up.at[h, g], up)
        send_on(1 + h, piece, 1, v_dn.at[h, g], dn)
        share_on(1 + h, piece, 0)

    def relay_v(h, g):
        relay(1 + h, vbs[h].at[rows_x(g, z_dn)], vbs[h].at[rows_x(g, z_up)],
              v_up.at[h, g], v_dn.at[h, g], v_far.at[h, g], g)

    def last_v(h, g):
        piece = vbs[h].at[rows_x(g, z_far)]
        arrived(piece, v_far.at[h, g])
        share_on(1 + h, piece, 3)

    own[0].wait()
    spread_k(0)

    def send_keys(k):
        px, py = back(k)
        push(k_in.at[:, :, lanes(py * 4 + px)], kb.at[my_rows], s1_send.at[0], k_recv.at[k], mesh_id(px, py, z, core))

    for k in (1, 2, 3, 4, 8, 12):
        send_keys(k)
    pl.semaphore_wait(row_in, 3)

    @pl.loop(0, 9)
    def _(n):
        send_keys(5 + lax.div(n, 3) * 4 + lax.rem(n, 3))

    def send_queries():
        @pl.loop(1, 16)
        def _(k):
            px, py = back(k)
            push(q_in.at[:, lanes(py * 4 + px)], qb.at[shares(k)], s1_send.at[1], q_recv, mesh_id(px, py, z, core))

    lane = lax.broadcasted_iota(jnp.int32, (1, DH), 1)
    low_half = lane < DH // 2

    def swap(a):
        return pltpu.roll(a, DH // 2, axis=1)

    def send_values():
        own[1].wait()

        @pl.loop(0, 16)
        def _(h):
            for blk in range(4):
                top = va[blk * BLK:blk * BLK + 32, lanes(h)].astype(jnp.float32)
                bottom = va[blk * BLK + 32:blk * BLK + 64, lanes(h)].astype(jnp.float32)
                vp[0, h, blk] = jnp.where(low_half, top, swap(bottom)).astype(jnp.bfloat16)
                vp[1, h, blk] = jnp.where(low_half, swap(top), bottom).astype(jnp.bfloat16)

        for h in range(2):
            pltpu.make_async_copy(vp.at[h, head], vbs[h].at[my_rows], v_recv.at[h, lax.div(x, 2)]).start()

            @pl.loop(1, 16)
            def _(k):
                px, py = back(k)
                push(vp.at[h, py * 4 + px], vbs[h].at[my_rows], s1_send.at[2 + h], v_recv.at[h, lax.div(k, 4) * 2 + lax.div(x, 2)],
                     mesh_id(px, py, z, core))

    def load_weight():
        for h in range(2):
            @pl.loop(0, 16)
            def _(k):
                px, py = back(k)
                pltpu.make_async_copy(
                    w_in.at[pl.ds(pl.multiple_of((py * 4 + px) * DH + h * 64, 64), 64)],
                    wv.at[h, pl.ds(pl.multiple_of(k * 64, 64), 64)], w_sem.at[h]).start()

    def blocks_of(g):
        found = []
        for i in range(GANG):
            px, py = peer(g * GANG + i)
            first = token_share(px, py, z, core) * 4
            for j in range(4):
                b = first + j
                found.append([
                    lax.rem(b + NB - 1, NB), b, lax.rem(b + 1, NB), 0, 1,
                    rand[0, b], rand[1, b], rand[2, b],
                ])
        return found

    def gang_rows(g, n):
        return pl.ds(pl.multiple_of(g * GANG * SHARE + n * BLK, BLK), BLK)

    def listed_keys(picks):
        blocks = [kb[pick] for pick in picks]
        return jnp.concatenate([b[0:32] for b in blocks] + [b[32:64] for b in blocks], axis=0)

    def weigh(g):
        scores = [
            lax.dot_general(qb[gang_rows(g, n), :], listed_keys(picks), (((1,), (1,)), ((), ())),
                            preferred_element_type=jnp.float32)
            for n, picks in enumerate(blocks_of(g))
        ]
        peaks = [jnp.max(s, axis=-1, keepdims=True) for s in scores]
        lifted = [jnp.exp2((s - peak) * EXP_SCALE) for s, peak in zip(scores, peaks)]
        scales = [1.0 / jnp.sum(e, axis=-1, keepdims=True) for e in lifted]
        for n, (e, scale) in enumerate(zip(lifted, scales)):
            pb[gang_rows(g, n), :] = (e * scale).astype(jnp.bfloat16)

    def attend(h, g):
        sums = []
        for n, picks in enumerate(blocks_of(g)):
            w = pb[gang_rows(g, n), :]
            w = jnp.concatenate([w[:, 0:256], w[:, 256:512]], axis=0)
            listed = jnp.concatenate([vbs[h][pick] for pick in picks], axis=0)
            sums.append(jnp.dot(w, listed, preferred_element_type=jnp.float32))
        outs = []
        for even, odd in zip(sums[0::2], sums[1::2]):
            outs.append(jnp.where(low_half, even[0:64] + swap(even[64:128]), swap(odd[0:64]) + odd[64:128]))
        ob[h, packed(g * GANG, GANG), :] = jnp.concatenate(outs, axis=0).astype(jnp.bfloat16)
        for i in range(GANG):
            k = g * GANG + i
            px, py = peer(k)

            @pl.when(k > 0)
            def _():
                push(ob.at[h, packed(k)], att.at[h, :, lanes(k)], ret_send.at[h], ret_recv.at[h], mesh_id(px, py, z, core))

            @pl.when(k == 0)
            def _():
                pltpu.make_async_copy(ob.at[h, packed(0)], att.at[h, :, pl.ds(0, DH)], ret_recv.at[h]).start()

    span = pl.ds(0, 64)
    half = pl.ds(0, 32)

    def at(i, begin, end):
        return (i >= begin) & (i < end)

    def at_eight(i, begin):
        return (i >= begin) & (i < begin + 8)

    @pl.loop(1, STOP)
    def _(i):
        @pl.when(i < 16)
        def _():
            arrived(kb.at[rows(i, z)], k_recv.at[i])
            spread_k(i)

        @pl.when(i == Q_AT)
        def _():
            send_queries()

        @pl.when(i == PACK_AT)
        def _():
            send_values()

        @pl.when(i == W_AT)
        def _():
            load_weight()

        for h in range(2):
            @pl.when(at_eight(i, V_AT[h]))
            def _():
                spread_v(h, i - V_AT[h])

        @pl.when(at(i, LAG, 16 + LAG))
        def _():
            relay_k(i - LAG)

        for h in range(2):
            @pl.when(at_eight(i, V_AT[h] + V_LAG))
            def _():
                relay_v(h, i - V_AT[h] - V_LAG)

        @pl.when(at(i, LAG_FAR, 16 + LAG_FAR))
        def _():
            last_k(i - LAG_FAR)

        for h in range(2):
            @pl.when(at_eight(i, V_AT[h] + V_FAR))
            def _():
                last_v(h, i - V_AT[h] - V_FAR)

        @pl.when(i == WEIGH_AT - 1)
        def _():
            own[2].wait()
            arrived(qb.at[shares(0, 15)], q_recv)
            for plane in range(4):
                arrived(kb.at[span], sib_recv.at[0, plane])

        @pl.when(at(i, WEIGH_AT, WEIGH_AT + 16 // GANG))
        def _():
            weigh(i - WEIGH_AT)

        @pl.when(i == FIRST_AT - 1)
        def _():
            for plane in range(4):
                arrived(vb0.at[span], sib_recv.at[1, plane])

        @pl.when(at(i, FIRST_AT, FIRST_AT + 16 // GANG))
        def _():
            attend(0, i - FIRST_AT)

    for plane in range(4):
        arrived(vb1.at[span], sib_recv.at[2, plane])

    @pl.loop(0, 16 // GANG)
    def _(g):
        attend(1, g)

    def unpack(h):
        for pair in range(8):
            a = att[h, :, 2 * pair * DH:(2 * pair + 1) * DH].astype(jnp.float32)
            b = att[h, :, (2 * pair + 1) * DH:(2 * pair + 2) * DH].astype(jnp.float32)
            cols = slice(h * 1024 + pair * DH, h * 1024 + (pair + 1) * DH)
            va[0:128, cols] = jnp.where(low_half, a, swap(b)).astype(jnp.bfloat16)
            va[128:256, cols] = jnp.where(low_half, swap(a), b).astype(jnp.bfloat16)

    def tile(n):
        return pl.ds(pl.multiple_of(n * TILE_N, TILE_N), TILE_N)

    arrived(wv.at[0], w_sem.at[0])
    arrived(ob.at[0], ret_recv.at[0])
    unpack(0)

    @pl.loop(0, D // TILE_N)
    def _(n):
        acc[:, tile(n)] = jnp.dot(va[:, 0:1024], wv[0, :, tile(n)], preferred_element_type=jnp.float32)

    arrived(wv.at[1], w_sem.at[1])
    arrived(ob.at[1], ret_recv.at[1])
    unpack(1)

    @pl.loop(0, D // TILE_N)
    def _(n):
        total = acc[:, tile(n)] + jnp.dot(va[:, 1024:2048], wv[1, :, tile(n)], preferred_element_type=jnp.float32)
        total = total.astype(jnp.bfloat16)
        done = jnp.concatenate([total[0:64], total[128:192], total[64:128], total[192:256]], axis=0)
        pb[shares(n), :] = done
        pltpu.make_async_copy(pb.at[shares(n)], out.at[:, tile(n)], out_sem).start()

    for i in range(2):
        arrived(ob.at[0, packed(0, 15)], ret_send.at[i])
        arrived(qb.at[shares(0, 15)], s1_send.at[i])
        arrived(ob.at[0, packed(0, 15)], s1_send.at[2 + i])
    for side, buf in enumerate((kb, vb0, vb1)):
        for i in range(2):
            arrived(buf.at[span], ring_send.at[side, i])
        for i in range(2, 4):
            arrived(buf.at[half], ring_send.at[side, i])
        for i in range(4):
            arrived(buf.at[span], sib_send.at[side, i])
    arrived(pb.at[shares(0, D // TILE_N)], out_sem)


def shards(queries, keys, values, rand_blocks, out_weight):
    any_spec = pl.BlockSpec(memory_space=pl.ANY)
    hbm = pl.BlockSpec(memory_space=pltpu.HBM)
    dma = pltpu.SemaphoreType.DMA
    return pl.pallas_call(
        kernel,
        out_shape=jax.ShapeDtypeStruct((SHARE, D), jnp.bfloat16),
        in_specs=[pl.BlockSpec(memory_space=pltpu.SMEM)] + [hbm] * 4,
        out_specs=any_spec,
        scratch_shapes=[
            pltpu.VMEM((NB, BLK, DH), jnp.bfloat16),
            pltpu.VMEM((NB, BLK // 2, DH), jnp.bfloat16),
            pltpu.VMEM((NB, BLK // 2, DH), jnp.bfloat16),
            pltpu.VMEM((16 * SHARE, DH), jnp.bfloat16),
            pltpu.VMEM((16 * SHARE, 8 * BLK), jnp.bfloat16),
            pltpu.VMEM((SHARE, H * DH), jnp.bfloat16),
            pltpu.VMEM((2, H, 4, BLK // 2, DH), jnp.bfloat16),
            pltpu.VMEM((2, 16 * SHARE // 2, DH), jnp.bfloat16),
            pltpu.VMEM((2, SHARE // 2, H * DH), jnp.bfloat16),
            pltpu.VMEM((2, H * DH // 2, D), jnp.bfloat16),
            pltpu.VMEM((SHARE, D), jnp.float32),
            dma((3,)), dma((4,)), dma((16,)), dma((2, 8)), dma,
            dma((16,)), dma((16,)), dma((16,)), dma((2, 8)), dma((2, 8)), dma((2, 8)),
            dma((3, 4)), dma((3, 4)), dma((3, 4)), dma((2,)), dma((2,)), dma((2,)), dma, pltpu.SemaphoreType.REGULAR,
        ],
        compiler_params=pltpu.CompilerParams(
            collective_id=0, has_side_effects=True, vmem_limit_bytes=VMEM_MIB * 1024 * 1024),
    )(rand_blocks.T, *[pltpu.with_memory_space_constraint(a, pltpu.HBM) for a in (queries, keys.reshape(4, BLK, H * DH), values, out_weight)])


def solution(mesh):
    return jax.shard_map(
        shards,
        mesh=mesh,
        in_specs=(
            P(("ctx", "ulys"), None),
            P(("ctx", "ulys"), None),
            P(("ctx", "ulys"), None),
            P(),
            P(),
        ),
        out_specs=P(("ctx", "ulys"), None),
        check_vma=False,
    )
```

```python
import functools

import jax
import jax.numpy as jnp
from jax import lax
from jax.experimental import pallas as pl
from jax.experimental.pallas import tpu as pltpu
from jax.sharding import PartitionSpec as P

H = 16
DH = 128
D = 4096
BLK = 64
NB = 512
TOKENS = 32768
SHARE = 256
MESH = pl.DeviceIdType.MESH
TILE_N = 512
LAG = 4
LAG_FAR = 9
V_AT = (16, 26)
V_LAG = 4
V_FAR = 8
Q_AT = 4
PACK_AT = 6
W_AT = 10
WEIGH_AT = 25
FIRST_AT = 32
STOP = 42
VMEM_MIB = 47
GANG = 2
EXP_SCALE = (DH ** -0.5) * 1.4426950408889634


def mesh_id(x, y, z, core):
    return ((lax.rem(z, 2) * 4 + y) * 2 + core, lax.div(z, 2) * 4 + x)


def token_share(x, y, z, core):
    ctx, ulys = mesh_id(x, y, z, core)
    return ctx * 8 + ulys


def kernel(rand_in, q_in, k_in, v_in, w_in, out,
           kb, vb0, vb1, qb, pb, va, vp, ob, att, wv, acc,
           own_sem, s1_send, k_recv, v_recv, q_recv, k_up, k_dn, k_far, v_up, v_dn, v_far,
           ring_send, sib_send, sib_recv, ret_send, ret_recv, w_sem, out_sem, row_in, rand):
    ctx, ulys = lax.axis_index("ctx"), lax.axis_index("ulys")
    core = lax.rem(ctx, 2)
    y = lax.rem(lax.div(ctx, 2), 4)
    z = lax.div(ulys, 4) * 2 + lax.div(ctx, 8)
    x = lax.rem(ulys, 4)
    head = y * 4 + x
    z_up, z_dn, z_far = lax.rem(z + 1, 4), lax.rem(z + 3, 4), lax.rem(z + 2, 4)
    up, dn = mesh_id(x, y, z_up, core), mesh_id(x, y, z_dn, core)
    sib = mesh_id(x, y, z, 1 - core)
    vbs = (vb0, vb1)

    def peer(k):
        return lax.rem(x + lax.rem(k, 4), 4), lax.rem(y + lax.div(k, 4), 4)

    def back(k):
        return lax.rem(x + 4 - lax.rem(k, 4), 4), lax.rem(y + 4 - lax.div(k, 4), 4)

    def lanes(h):
        return pl.ds(pl.multiple_of(h * DH, DH), DH)

    def rows(k, zz):
        px, py = peer(k)
        return pl.ds(token_share(px, py, zz, core) * 4, 4)

    def rows_x(g, zz):
        return pl.ds(token_share(lax.rem(g, 2) * 2, lax.rem(y + lax.div(g, 2), 4), zz, core) * 4, 8)

    def shares(k, count=1):
        return pl.ds(pl.multiple_of(k * SHARE, SHARE), count * SHARE)

    def packed(k, count=1):
        return pl.ds(pl.multiple_of(k * DH, DH), count * DH)

    my_rows = rows(0, z)
    own = [
        pltpu.make_async_copy(rand_in, rand, own_sem.at[3]),
        pltpu.make_async_copy(k_in.at[:, :, lanes(head)], kb.at[my_rows], own_sem.at[0]),
        pltpu.make_async_copy(v_in, va, own_sem.at[1]),
        pltpu.make_async_copy(q_in.at[:, lanes(head)], qb.at[shares(0)], own_sem.at[2]),
    ]
    for copy in own:
        copy.start()

    barrier = pltpu.get_barrier_semaphore()
    for device in (up, dn, sib):
        pl.semaphore_signal(barrier, inc=1, device_id=device, device_id_type=MESH)
    for k in (1, 2, 3, 4, 8, 12):
        px, py = back(k)
        pl.semaphore_signal(barrier, inc=1, device_id=mesh_id(px, py, z, core), device_id_type=MESH)
    pl.semaphore_wait(barrier, 9)
    for k in (4, 8, 12):
        px, py = back(k)
        pl.semaphore_signal(row_in, inc=1, device_id=mesh_id(px, py, z, core), device_id_type=MESH)

    def push(src, dst, send, recv, device):
        pltpu.make_async_remote_copy(
            src_ref=src, dst_ref=dst, send_sem=send, recv_sem=recv,
            device_id=device, device_id_type=MESH).start()

    def arrived(piece, sem):
        pltpu.make_async_copy(piece, piece, sem).wait()

    def send_on(side, piece, via, sem, device):
        push(piece, piece, ring_send.at[side, via], sem, device)

    def share_on(side, piece, plane):
        push(piece, piece, sib_send.at[side, plane], sib_recv.at[side, plane], sib)

    def relay(side, low, high, from_low, from_high, to_far, k):
        arrived(low, from_low)

        @pl.when(lax.rem(k, 2) == 0)
        def _():
            send_on(side, low, 2, to_far, up)
        share_on(side, low, 1)
        arrived(high, from_high)

        @pl.when(lax.rem(k, 2) == 1)
        def _():
            send_on(side, high, 3, to_far, dn)
        share_on(side, high, 2)

    def spread_k(k):
        piece = kb.at[rows(k, z)]
        send_on(0, piece, 0, k_up.at[k], up)
        send_on(0, piece, 1, k_dn.at[k], dn)
        share_on(0, piece, 0)

    def relay_k(k):
        relay(0, kb.at[rows(k, z_dn)], kb.at[rows(k, z_up)], k_up.at[k], k_dn.at[k], k_far.at[k], k)

    def last_k(k):
        piece = kb.at[rows(k, z_far)]
        arrived(piece, k_far.at[k])
        share_on(0, piece, 3)

    def spread_v(h, g):
        piece = vbs[h].at[rows_x(g, z)]
        arrived(piece, v_recv.at[h, g])
        send_on(1 + h, piece, 0, v_up.at[h, g], up)
        send_on(1 + h, piece, 1, v_dn.at[h, g], dn)
        share_on(1 + h, piece, 0)

    def relay_v(h, g):
        relay(1 + h, vbs[h].at[rows_x(g, z_dn)], vbs[h].at[rows_x(g, z_up)],
              v_up.at[h, g], v_dn.at[h, g], v_far.at[h, g], g)

    def last_v(h, g):
        piece = vbs[h].at[rows_x(g, z_far)]
        arrived(piece, v_far.at[h, g])
        share_on(1 + h, piece, 3)

    own[1].wait()
    spread_k(0)

    def send_keys(k):
        px, py = back(k)
        push(k_in.at[:, :, lanes(py * 4 + px)], kb.at[my_rows], s1_send.at[0], k_recv.at[k], mesh_id(px, py, z, core))

    for k in (1, 2, 3, 4, 8, 12):
        send_keys(k)
    pl.semaphore_wait(row_in, 3)

    @pl.loop(0, 9)
    def _(n):
        send_keys(5 + lax.div(n, 3) * 4 + lax.rem(n, 3))

    def send_queries():
        @pl.loop(1, 16)
        def _(k):
            px, py = back(k)
            push(q_in.at[:, lanes(py * 4 + px)], qb.at[shares(k)], s1_send.at[1], q_recv, mesh_id(px, py, z, core))

    lane = lax.broadcasted_iota(jnp.int32, (1, DH), 1)
    low_half = lane < DH // 2

    def swap(a):
        return pltpu.roll(a, DH // 2, axis=1)

    def send_values():
        own[2].wait()

        @pl.loop(0, 16)
        def _(h):
            for blk in range(4):
                top = va[blk * BLK:blk * BLK + 32, lanes(h)].astype(jnp.float32)
                bottom = va[blk * BLK + 32:blk * BLK + 64, lanes(h)].astype(jnp.float32)
                vp[0, h, blk] = jnp.where(low_half, top, swap(bottom)).astype(jnp.bfloat16)
                vp[1, h, blk] = jnp.where(low_half, swap(top), bottom).astype(jnp.bfloat16)

        for h in range(2):
            pltpu.make_async_copy(vp.at[h, head], vbs[h].at[my_rows], v_recv.at[h, lax.div(x, 2)]).start()

            @pl.loop(1, 16)
            def _(k):
                px, py = back(k)
                push(vp.at[h, py * 4 + px], vbs[h].at[my_rows], s1_send.at[2 + h], v_recv.at[h, lax.div(k, 4) * 2 + lax.div(x, 2)],
                     mesh_id(px, py, z, core))

    def load_weight():
        for h in range(2):
            @pl.loop(0, 16)
            def _(k):
                px, py = back(k)
                pltpu.make_async_copy(
                    w_in.at[pl.ds(pl.multiple_of((py * 4 + px) * DH + h * 64, 64), 64)],
                    wv.at[h, pl.ds(pl.multiple_of(k * 64, 64), 64)], w_sem.at[h]).start()

    def blocks_of(g):
        found = []
        for i in range(GANG):
            px, py = peer(g * GANG + i)
            first = token_share(px, py, z, core) * 4
            for j in range(4):
                b = first + j
                found.append([
                    lax.rem(b + NB - 1, NB), b, lax.rem(b + 1, NB), 0, 1,
                    rand[0, b], rand[1, b], rand[2, b],
                ])
        return found

    def gang_rows(g, n):
        return pl.ds(pl.multiple_of(g * GANG * SHARE + n * BLK, BLK), BLK)

    def listed_keys(picks):
        blocks = [kb[pick] for pick in picks]
        return jnp.concatenate([b[0:32] for b in blocks] + [b[32:64] for b in blocks], axis=0)

    def weigh(g):
        scores = [
            lax.dot_general(qb[gang_rows(g, n), :], listed_keys(picks), (((1,), (1,)), ((), ())),
                            preferred_element_type=jnp.float32)
            for n, picks in enumerate(blocks_of(g))
        ]
        peaks = [jnp.max(s, axis=-1, keepdims=True) for s in scores]
        lifted = [jnp.exp2((s - peak) * EXP_SCALE) for s, peak in zip(scores, peaks)]
        scales = [1.0 / jnp.sum(e, axis=-1, keepdims=True) for e in lifted]
        for n, (e, scale) in enumerate(zip(lifted, scales)):
            pb[gang_rows(g, n), :] = (e * scale).astype(jnp.bfloat16)

    def attend(h, g):
        sums = []
        for n, picks in enumerate(blocks_of(g)):
            w = pb[gang_rows(g, n), :]
            w = jnp.concatenate([w[:, 0:256], w[:, 256:512]], axis=0)
            listed = jnp.concatenate([vbs[h][pick] for pick in picks], axis=0)
            sums.append(jnp.dot(w, listed, preferred_element_type=jnp.float32))
        outs = []
        for even, odd in zip(sums[0::2], sums[1::2]):
            outs.append(jnp.where(low_half, even[0:64] + swap(even[64:128]), swap(odd[0:64]) + odd[64:128]))
        ob[h, packed(g * GANG, GANG), :] = jnp.concatenate(outs, axis=0).astype(jnp.bfloat16)
        for i in range(GANG):
            k = g * GANG + i
            px, py = peer(k)

            @pl.when(k > 0)
            def _():
                push(ob.at[h, packed(k)], att.at[h, :, lanes(k)], ret_send.at[h], ret_recv.at[h + h * lax.div(k, 8)], mesh_id(px, py, z, core))

            @pl.when(k == 0)
            def _():
                pltpu.make_async_copy(ob.at[h, packed(0)], att.at[h, :, pl.ds(0, DH)], ret_recv.at[h]).start()

    span = pl.ds(0, 64)
    half = pl.ds(0, 32)

    def at(i, begin, end):
        return (i >= begin) & (i < end)

    def at_eight(i, begin):
        return (i >= begin) & (i < begin + 8)

    @pl.loop(1, STOP)
    def _(i):
        @pl.when(i < 16)
        def _():
            arrived(kb.at[rows(i, z)], k_recv.at[i])
            spread_k(i)

        @pl.when(i == Q_AT)
        def _():
            send_queries()

        @pl.when(i == PACK_AT)
        def _():
            send_values()

        @pl.when(i == W_AT)
        def _():
            load_weight()

        for h in range(2):
            @pl.when(at_eight(i, V_AT[h]))
            def _():
                spread_v(h, i - V_AT[h])

        @pl.when(at(i, LAG, 16 + LAG))
        def _():
            relay_k(i - LAG)

        for h in range(2):
            @pl.when(at_eight(i, V_AT[h] + V_LAG))
            def _():
                relay_v(h, i - V_AT[h] - V_LAG)

        @pl.when(at(i, LAG_FAR, 16 + LAG_FAR))
        def _():
            last_k(i - LAG_FAR)

        for h in range(2):
            @pl.when(at_eight(i, V_AT[h] + V_FAR))
            def _():
                last_v(h, i - V_AT[h] - V_FAR)

        @pl.when(i == WEIGH_AT - 1)
        def _():
            own[0].wait()
            own[3].wait()
            arrived(qb.at[shares(0, 15)], q_recv)
            for plane in range(4):
                arrived(kb.at[span], sib_recv.at[0, plane])

        @pl.when(at(i, WEIGH_AT, WEIGH_AT + 16 // GANG))
        def _():
            weigh(i - WEIGH_AT)

        @pl.when(i == FIRST_AT - 1)
        def _():
            for plane in range(4):
                arrived(vb0.at[span], sib_recv.at[1, plane])

        @pl.when(at(i, FIRST_AT, FIRST_AT + 16 // GANG))
        def _():
            attend(0, i - FIRST_AT)

    for plane in range(4):
        arrived(vb1.at[span], sib_recv.at[2, plane])

    @pl.loop(0, 16 // GANG)
    def _(g):
        attend(1, g)

    def unpack(h, begin, end):
        for pair in range(begin, end):
            a = att[h, :, 2 * pair * DH:(2 * pair + 1) * DH].astype(jnp.float32)
            b = att[h, :, (2 * pair + 1) * DH:(2 * pair + 2) * DH].astype(jnp.float32)
            cols = slice(h * 1024 + pair * DH, h * 1024 + (pair + 1) * DH)
            va[0:128, cols] = jnp.where(low_half, a, swap(b)).astype(jnp.bfloat16)
            va[128:256, cols] = jnp.where(low_half, swap(a), b).astype(jnp.bfloat16)

    def tile(n):
        return pl.ds(pl.multiple_of(n * TILE_N, TILE_N), TILE_N)

    arrived(wv.at[0], w_sem.at[0])
    arrived(ob.at[0], ret_recv.at[0])
    unpack(0, 0, 8)

    @pl.loop(0, D // TILE_N)
    def _(n):
        acc[:, tile(n)] = jnp.dot(va[:, 0:1024], wv[0, :, tile(n)], preferred_element_type=jnp.float32)

    arrived(wv.at[1], w_sem.at[1])
    arrived(ob.at[1, packed(0, 8)], ret_recv.at[1])
    unpack(1, 0, 4)

    @pl.loop(0, D // TILE_N)
    def _(n):
        acc[:, tile(n)] += jnp.dot(va[:, 1024:1536], wv[1, 0:512, tile(n)], preferred_element_type=jnp.float32)

    arrived(ob.at[1, packed(0, 8)], ret_recv.at[2])
    unpack(1, 4, 8)

    @pl.loop(0, D // TILE_N)
    def _(n):
        total = acc[:, tile(n)] + jnp.dot(va[:, 1536:2048], wv[1, 512:1024, tile(n)], preferred_element_type=jnp.float32)
        total = total.astype(jnp.bfloat16)
        done = jnp.concatenate([total[0:64], total[128:192], total[64:128], total[192:256]], axis=0)
        pb[shares(n), :] = done
        pltpu.make_async_copy(pb.at[shares(n)], out.at[:, tile(n)], out_sem).start()

    for i in range(2):
        arrived(ob.at[0, packed(0, 15)], ret_send.at[i])
        arrived(qb.at[shares(0, 15)], s1_send.at[i])
        arrived(ob.at[0, packed(0, 15)], s1_send.at[2 + i])
    for side, buf in enumerate((kb, vb0, vb1)):
        for i in range(2):
            arrived(buf.at[span], ring_send.at[side, i])
        for i in range(2, 4):
            arrived(buf.at[half], ring_send.at[side, i])
        for i in range(4):
            arrived(buf.at[span], sib_send.at[side, i])
    arrived(pb.at[shares(0, D // TILE_N)], out_sem)


def shards(queries, keys, values, rand_blocks, out_weight):
    any_spec = pl.BlockSpec(memory_space=pl.ANY)
    hbm = pl.BlockSpec(memory_space=pltpu.HBM)
    dma = pltpu.SemaphoreType.DMA
    return pl.pallas_call(
        kernel,
        out_shape=jax.ShapeDtypeStruct((SHARE, D), jnp.bfloat16),
        in_specs=[hbm] * 5,
        out_specs=any_spec,
        scratch_shapes=[
            pltpu.VMEM((NB, BLK, DH), jnp.bfloat16),
            pltpu.VMEM((NB, BLK // 2, DH), jnp.bfloat16),
            pltpu.VMEM((NB, BLK // 2, DH), jnp.bfloat16),
            pltpu.VMEM((16 * SHARE, DH), jnp.bfloat16),
            pltpu.VMEM((16 * SHARE, 8 * BLK), jnp.bfloat16),
            pltpu.VMEM((SHARE, H * DH), jnp.bfloat16),
            pltpu.VMEM((2, H, 4, BLK // 2, DH), jnp.bfloat16),
            pltpu.VMEM((2, 16 * SHARE // 2, DH), jnp.bfloat16),
            pltpu.VMEM((2, SHARE // 2, H * DH), jnp.bfloat16),
            pltpu.VMEM((2, H * DH // 2, D), jnp.bfloat16),
            pltpu.VMEM((SHARE, D), jnp.float32),
            dma((4,)), dma((4,)), dma((16,)), dma((2, 8)), dma,
            dma((16,)), dma((16,)), dma((16,)), dma((2, 8)), dma((2, 8)), dma((2, 8)),
            dma((3, 4)), dma((3, 4)), dma((3, 4)), dma((2,)), dma((3,)), dma((2,)), dma, pltpu.SemaphoreType.REGULAR,
            pltpu.SMEM((3, NB), jnp.int32),
        ],
        compiler_params=pltpu.CompilerParams(
            collective_id=0, has_side_effects=True, vmem_limit_bytes=VMEM_MIB * 1024 * 1024),
    )(*[pltpu.with_memory_space_constraint(a, pltpu.HBM) for a in (rand_blocks.T, queries, keys.reshape(4, BLK, H * DH), values, out_weight)])


def solution(mesh):
    return jax.shard_map(
        shards,
        mesh=mesh,
        in_specs=(
            P(("ctx", "ulys"), None),
            P(("ctx", "ulys"), None),
            P(("ctx", "ulys"), None),
            P(),
            P(),
        ),
        out_specs=P(("ctx", "ulys"), None),
        check_vma=False,
    )
```

```python
import functools

import jax
import jax.numpy as jnp
from jax import lax
from jax.experimental import pallas as pl
from jax.experimental.pallas import tpu as pltpu
from jax.sharding import PartitionSpec as P

H = 16
DH = 128
D = 4096
BLK = 64
NB = 512
TOKENS = 32768
SHARE = 256
MESH = pl.DeviceIdType.MESH
TILE_N = 512
LAG = 4
LAG_FAR = 9
V_AT = (16, 27)
V_LAG = 4
V_FAR = 8
Q_AT = 4
PACK_AT = 6
W_AT = 10
WEIGH_AT = 25
FIRST_AT = 32
PART = 8
STOP = 43
VMEM_MIB = 47
GANG = 2
EXP_SCALE = (DH ** -0.5) * 1.4426950408889634


def mesh_id(x, y, z, core):
    return ((lax.rem(z, 2) * 4 + y) * 2 + core, lax.div(z, 2) * 4 + x)


def token_share(x, y, z, core):
    ctx, ulys = mesh_id(x, y, z, core)
    return ctx * 8 + ulys


def kernel(rand_in, q_in, k_in, v_in, w_in, out,
           kb, vb0, vb1, qb, pb, va, vp, ob, att, wv, acc,
           own_sem, s1_send, k_recv, v_recv, q_recv, k_up, k_dn, k_far, v_up, v_dn, v_far,
           ring_send, sib_send, sib_recv, ret_send, ret_recv, w_sem, out_sem, row_in, rand):
    ctx, ulys = lax.axis_index("ctx"), lax.axis_index("ulys")
    core = lax.rem(ctx, 2)
    y = lax.rem(lax.div(ctx, 2), 4)
    z = lax.div(ulys, 4) * 2 + lax.div(ctx, 8)
    x = lax.rem(ulys, 4)
    head = y * 4 + x
    z_up, z_dn, z_far = lax.rem(z + 1, 4), lax.rem(z + 3, 4), lax.rem(z + 2, 4)
    up, dn = mesh_id(x, y, z_up, core), mesh_id(x, y, z_dn, core)
    sib = mesh_id(x, y, z, 1 - core)
    vbs = (vb0, vb1)

    def peer(k):
        return lax.rem(x + lax.rem(k, 4), 4), lax.rem(y + lax.div(k, 4), 4)

    def back(k):
        return lax.rem(x + 4 - lax.rem(k, 4), 4), lax.rem(y + 4 - lax.div(k, 4), 4)

    def lanes(h):
        return pl.ds(pl.multiple_of(h * DH, DH), DH)

    def rows(k, zz):
        px, py = peer(k)
        return pl.ds(token_share(px, py, zz, core) * 4, 4)

    def rows_x(g, zz):
        return pl.ds(token_share(lax.rem(g, 2) * 2, lax.rem(y + lax.div(g, 2), 4), zz, core) * 4, 8)

    def shares(k, count=1):
        return pl.ds(pl.multiple_of(k * SHARE, SHARE), count * SHARE)

    def packed(k, count=1):
        return pl.ds(pl.multiple_of(k * DH, DH), count * DH)

    my_rows = rows(0, z)
    own = [
        pltpu.make_async_copy(rand_in, rand, own_sem.at[3]),
        pltpu.make_async_copy(k_in.at[:, :, lanes(head)], kb.at[my_rows], own_sem.at[0]),
        pltpu.make_async_copy(v_in, va, own_sem.at[1]),
        pltpu.make_async_copy(q_in.at[:, lanes(head)], qb.at[shares(0)], own_sem.at[2]),
    ]
    barrier = pltpu.get_barrier_semaphore()
    for device in (up, dn, sib):
        pl.semaphore_signal(barrier, inc=1, device_id=device, device_id_type=MESH)
    for k in (1, 2, 3, 4, 8, 12):
        px, py = back(k)
        pl.semaphore_signal(barrier, inc=1, device_id=mesh_id(px, py, z, core), device_id_type=MESH)
    for copy in own:
        copy.start()
    pl.semaphore_wait(barrier, 9)
    for k in (4, 8, 12):
        px, py = back(k)
        pl.semaphore_signal(row_in, inc=1, device_id=mesh_id(px, py, z, core), device_id_type=MESH)

    def push(src, dst, send, recv, device):
        pltpu.make_async_remote_copy(
            src_ref=src, dst_ref=dst, send_sem=send, recv_sem=recv,
            device_id=device, device_id_type=MESH).start()

    def arrived(piece, sem):
        pltpu.make_async_copy(piece, piece, sem).wait()

    def send_on(side, piece, via, sem, device):
        push(piece, piece, ring_send.at[side, via], sem, device)

    def share_on(side, piece, plane):
        push(piece, piece, sib_send.at[side, plane], sib_recv.at[side, plane], sib)

    def relay(side, low, high, from_low, from_high, to_far, k):
        arrived(low, from_low)

        @pl.when(lax.rem(k, 2) == 0)
        def _():
            send_on(side, low, 2, to_far, up)
        share_on(side, low, 1)
        arrived(high, from_high)

        @pl.when(lax.rem(k, 2) == 1)
        def _():
            send_on(side, high, 3, to_far, dn)
        share_on(side, high, 2)

    def spread_k(k):
        piece = kb.at[rows(k, z)]
        send_on(0, piece, 0, k_up.at[k], up)
        send_on(0, piece, 1, k_dn.at[k], dn)
        share_on(0, piece, 0)

    def relay_k(k):
        relay(0, kb.at[rows(k, z_dn)], kb.at[rows(k, z_up)], k_up.at[k], k_dn.at[k], k_far.at[k], k)

    def last_k(k):
        piece = kb.at[rows(k, z_far)]
        arrived(piece, k_far.at[k])
        share_on(0, piece, 3)

    def spread_v(h, g):
        piece = vbs[h].at[rows_x(g, z)]
        arrived(piece, v_recv.at[h, g])
        send_on(1 + h, piece, 0, v_up.at[h, g], up)
        send_on(1 + h, piece, 1, v_dn.at[h, g], dn)
        share_on(1 + h, piece, 0)

    def relay_v(h, g):
        relay(1 + h, vbs[h].at[rows_x(g, z_dn)], vbs[h].at[rows_x(g, z_up)],
              v_up.at[h, g], v_dn.at[h, g], v_far.at[h, g], g)

    def last_v(h, g):
        piece = vbs[h].at[rows_x(g, z_far)]
        arrived(piece, v_far.at[h, g])
        share_on(1 + h, piece, 3)

    own[1].wait()
    spread_k(0)

    def send_keys(k):
        px, py = back(k)
        push(k_in.at[:, :, lanes(py * 4 + px)], kb.at[my_rows], s1_send.at[0], k_recv.at[k], mesh_id(px, py, z, core))

    for k in (1, 2, 3, 4, 8, 12):
        send_keys(k)
    pl.semaphore_wait(row_in, 3)

    @pl.loop(0, 9)
    def _(n):
        send_keys(5 + lax.div(n, 3) * 4 + lax.rem(n, 3))

    def send_queries():
        @pl.loop(1, 16)
        def _(k):
            px, py = back(k)
            push(q_in.at[:, lanes(py * 4 + px)], qb.at[shares(k)], s1_send.at[1], q_recv, mesh_id(px, py, z, core))

    lane = lax.broadcasted_iota(jnp.int32, (1, DH), 1)
    low_half = lane < DH // 2

    def swap(a):
        return pltpu.roll(a, DH // 2, axis=1)

    def send_values():
        own[2].wait()

        @pl.loop(0, 16)
        def _(h):
            for blk in range(4):
                top = va[blk * BLK:blk * BLK + 32, lanes(h)].astype(jnp.float32)
                bottom = va[blk * BLK + 32:blk * BLK + 64, lanes(h)].astype(jnp.float32)
                vp[0, h, blk] = jnp.where(low_half, top, swap(bottom)).astype(jnp.bfloat16)
                vp[1, h, blk] = jnp.where(low_half, swap(top), bottom).astype(jnp.bfloat16)

        for h in range(2):
            pltpu.make_async_copy(vp.at[h, head], vbs[h].at[my_rows], v_recv.at[h, lax.div(x, 2)]).start()

            @pl.loop(1, 16)
            def _(k):
                px, py = back(k)
                push(vp.at[h, py * 4 + px], vbs[h].at[my_rows], s1_send.at[2 + h], v_recv.at[h, lax.div(k, 4) * 2 + lax.div(x, 2)],
                     mesh_id(px, py, z, core))

    def load_weight():
        for h in range(2):
            @pl.loop(0, 16)
            def _(k):
                px, py = back(k)
                pltpu.make_async_copy(
                    w_in.at[pl.ds(pl.multiple_of((py * 4 + px) * DH + h * 64, 64), 64)],
                    wv.at[h, pl.ds(pl.multiple_of(k * 64, 64), 64)], w_sem.at[h]).start()

    def blocks_of(g):
        found = []
        for i in range(GANG):
            px, py = peer(g * GANG + i)
            first = token_share(px, py, z, core) * 4
            for j in range(4):
                b = first + j
                found.append([
                    lax.rem(b + NB - 1, NB), b, lax.rem(b + 1, NB), 0, 1,
                    rand[0, b], rand[1, b], rand[2, b],
                ])
        return found

    def gang_rows(g, n):
        return pl.ds(pl.multiple_of(g * GANG * SHARE + n * BLK, BLK), BLK)

    def listed_keys(picks):
        blocks = [kb[pick] for pick in picks]
        return jnp.concatenate([b[0:32] for b in blocks] + [b[32:64] for b in blocks], axis=0)

    def weigh(g):
        scores = [
            lax.dot_general(qb[gang_rows(g, n), :], listed_keys(picks), (((1,), (1,)), ((), ())),
                            preferred_element_type=jnp.float32)
            for n, picks in enumerate(blocks_of(g))
        ]
        peaks = [jnp.max(s, axis=-1, keepdims=True) for s in scores]
        lifted = [jnp.exp2((s - peak) * EXP_SCALE) for s, peak in zip(scores, peaks)]
        scales = [1.0 / jnp.sum(e, axis=-1, keepdims=True) for e in lifted]
        for n, (e, scale) in enumerate(zip(lifted, scales)):
            pb[gang_rows(g, n), :] = (e * scale).astype(jnp.bfloat16)

    def attend(h, g):
        sums = []
        for n, picks in enumerate(blocks_of(g)):
            w = pb[gang_rows(g, n), :]
            w = jnp.concatenate([w[:, 0:256], w[:, 256:512]], axis=0)
            listed = jnp.concatenate([vbs[h][pick] for pick in picks], axis=0)
            sums.append(jnp.dot(w, listed, preferred_element_type=jnp.float32))
        outs = []
        for even, odd in zip(sums[0::2], sums[1::2]):
            outs.append(jnp.where(low_half, even[0:64] + swap(even[64:128]), swap(odd[0:64]) + odd[64:128]))
        ob[h, packed(g * GANG, GANG), :] = jnp.concatenate(outs, axis=0).astype(jnp.bfloat16)
        for i in range(GANG):
            k = g * GANG + i
            px, py = peer(k)

            @pl.when(k > 0)
            def _():
                push(ob.at[h, packed(k)], att.at[h, :, lanes(k)], ret_send.at[h], ret_recv.at[h + h * lax.div(k, PART)], mesh_id(px, py, z, core))

            @pl.when(k == 0)
            def _():
                pltpu.make_async_copy(ob.at[h, packed(0)], att.at[h, :, pl.ds(0, DH)], ret_recv.at[h]).start()

    span = pl.ds(0, 64)
    half = pl.ds(0, 32)

    def at(i, begin, end):
        return (i >= begin) & (i < end)

    def at_eight(i, begin):
        return (i >= begin) & (i < begin + 8)

    @pl.loop(1, STOP)
    def _(i):
        @pl.when(i < 16)
        def _():
            arrived(kb.at[rows(i, z)], k_recv.at[i])
            spread_k(i)

        @pl.when(i == Q_AT)
        def _():
            send_queries()

        @pl.when(i == PACK_AT)
        def _():
            send_values()

        @pl.when(i == W_AT)
        def _():
            load_weight()

        for h in range(2):
            @pl.when(at_eight(i, V_AT[h]))
            def _():
                spread_v(h, i - V_AT[h])

        @pl.when(at(i, LAG, 16 + LAG))
        def _():
            relay_k(i - LAG)

        for h in range(2):
            @pl.when(at_eight(i, V_AT[h] + V_LAG))
            def _():
                relay_v(h, i - V_AT[h] - V_LAG)

        @pl.when(at(i, LAG_FAR, 16 + LAG_FAR))
        def _():
            last_k(i - LAG_FAR)

        for h in range(2):
            @pl.when(at_eight(i, V_AT[h] + V_FAR))
            def _():
                last_v(h, i - V_AT[h] - V_FAR)

        @pl.when(i == WEIGH_AT - 1)
        def _():
            own[0].wait()
            own[3].wait()
            arrived(qb.at[shares(0, 15)], q_recv)
            for plane in range(4):
                arrived(kb.at[span], sib_recv.at[0, plane])

        @pl.when(at(i, WEIGH_AT, WEIGH_AT + 16 // GANG))
        def _():
            weigh(i - WEIGH_AT)

        @pl.when(i == FIRST_AT - 1)
        def _():
            for plane in range(4):
                arrived(vb0.at[span], sib_recv.at[1, plane])

        @pl.when(at(i, FIRST_AT, FIRST_AT + 16 // GANG))
        def _():
            attend(0, i - FIRST_AT)

    for plane in range(4):
        arrived(vb1.at[span], sib_recv.at[2, plane])

    @pl.loop(0, 16 // GANG)
    def _(g):
        attend(1, g)

    def unpack(h, begin, end):
        for pair in range(begin, end):
            a = att[h, :, 2 * pair * DH:(2 * pair + 1) * DH].astype(jnp.float32)
            b = att[h, :, (2 * pair + 1) * DH:(2 * pair + 2) * DH].astype(jnp.float32)
            cols = slice(h * 1024 + pair * DH, h * 1024 + (pair + 1) * DH)
            va[0:128, cols] = jnp.where(low_half, a, swap(b)).astype(jnp.bfloat16)
            va[128:256, cols] = jnp.where(low_half, swap(a), b).astype(jnp.bfloat16)

    def tile(n):
        return pl.ds(pl.multiple_of(n * TILE_N, TILE_N), TILE_N)

    arrived(wv.at[0], w_sem.at[0])
    arrived(ob.at[0], ret_recv.at[0])
    unpack(0, 0, 8)

    @pl.loop(0, D // TILE_N)
    def _(n):
        acc[:, tile(n)] = jnp.dot(va[:, 0:1024], wv[0, :, tile(n)], preferred_element_type=jnp.float32)

    arrived(wv.at[1], w_sem.at[1])
    arrived(ob.at[1, packed(0, PART)], ret_recv.at[1])
    unpack(1, 0, PART // 2)

    @pl.loop(0, D // TILE_N)
    def _(n):
        acc[:, tile(n)] += jnp.dot(va[:, 1024:1024 + PART * 64], wv[1, 0:PART * 64, tile(n)], preferred_element_type=jnp.float32)

    arrived(ob.at[1, packed(0, 16 - PART)], ret_recv.at[2])
    unpack(1, PART // 2, 8)

    @pl.loop(0, D // TILE_N)
    def _(n):
        total = acc[:, tile(n)] + jnp.dot(va[:, 1024 + PART * 64:2048], wv[1, PART * 64:1024, tile(n)], preferred_element_type=jnp.float32)
        total = total.astype(jnp.bfloat16)
        done = jnp.concatenate([total[0:64], total[128:192], total[64:128], total[192:256]], axis=0)
        pb[shares(n), :] = done
        pltpu.make_async_copy(pb.at[shares(n)], out.at[:, tile(n)], out_sem).start()

    for i in range(2):
        arrived(ob.at[0, packed(0, 15)], ret_send.at[i])
        arrived(qb.at[shares(0, 15)], s1_send.at[i])
        arrived(ob.at[0, packed(0, 15)], s1_send.at[2 + i])
    for side, buf in enumerate((kb, vb0, vb1)):
        for i in range(2):
            arrived(buf.at[span], ring_send.at[side, i])
        for i in range(2, 4):
            arrived(buf.at[half], ring_send.at[side, i])
        for i in range(4):
            arrived(buf.at[span], sib_send.at[side, i])
    arrived(pb.at[shares(0, D // TILE_N)], out_sem)


def shards(queries, keys, values, rand_blocks, out_weight):
    any_spec = pl.BlockSpec(memory_space=pl.ANY)
    hbm = pl.BlockSpec(memory_space=pltpu.HBM)
    dma = pltpu.SemaphoreType.DMA
    return pl.pallas_call(
        kernel,
        out_shape=jax.ShapeDtypeStruct((SHARE, D), jnp.bfloat16),
        in_specs=[hbm] * 5,
        out_specs=any_spec,
        scratch_shapes=[
            pltpu.VMEM((NB, BLK, DH), jnp.bfloat16),
            pltpu.VMEM((NB, BLK // 2, DH), jnp.bfloat16),
            pltpu.VMEM((NB, BLK // 2, DH), jnp.bfloat16),
            pltpu.VMEM((16 * SHARE, DH), jnp.bfloat16),
            pltpu.VMEM((16 * SHARE, 8 * BLK), jnp.bfloat16),
            pltpu.VMEM((SHARE, H * DH), jnp.bfloat16),
            pltpu.VMEM((2, H, 4, BLK // 2, DH), jnp.bfloat16),
            pltpu.VMEM((2, 16 * SHARE // 2, DH), jnp.bfloat16),
            pltpu.VMEM((2, SHARE // 2, H * DH), jnp.bfloat16),
            pltpu.VMEM((2, H * DH // 2, D), jnp.bfloat16),
            pltpu.VMEM((SHARE, D), jnp.float32),
            dma((4,)), dma((4,)), dma((16,)), dma((2, 8)), dma,
            dma((16,)), dma((16,)), dma((16,)), dma((2, 8)), dma((2, 8)), dma((2, 8)),
            dma((3, 4)), dma((3, 4)), dma((3, 4)), dma((2,)), dma((3,)), dma((2,)), dma, pltpu.SemaphoreType.REGULAR,
            pltpu.SMEM((3, NB), jnp.int32),
        ],
        compiler_params=pltpu.CompilerParams(
            collective_id=0, has_side_effects=True, vmem_limit_bytes=VMEM_MIB * 1024 * 1024),
    )(*[pltpu.with_memory_space_constraint(a, pltpu.HBM) for a in (rand_blocks.T, queries, keys.reshape(4, BLK, H * DH), values, out_weight)])


def solution(mesh):
    return jax.shard_map(
        shards,
        mesh=mesh,
        in_specs=(
            P(("ctx", "ulys"), None),
            P(("ctx", "ulys"), None),
            P(("ctx", "ulys"), None),
            P(),
            P(),
        ),
        out_specs=P(("ctx", "ulys"), None),
        check_vma=False,
    )
```

```python
import functools

import jax
import jax.numpy as jnp
from jax import lax
from jax.experimental import pallas as pl
from jax.experimental.pallas import tpu as pltpu
from jax.sharding import PartitionSpec as P

H = 16
DH = 128
D = 4096
BLK = 64
NB = 512
TOKENS = 32768
SHARE = 256
MESH = pl.DeviceIdType.MESH
TILE_N = 512
LAG = 4
LAG_FAR = 9
V_AT = (16, 27)
V_LAG = 4
V_FAR = 8
Q_AT = 4
PACK_AT = 6
W_AT = 10
WEIGH_AT = 25
FIRST_AT = 32
PART = 6
STOP = 43
VMEM_MIB = 47
GANG = 2
EXP_SCALE = (DH ** -0.5) * 1.4426950408889634


def mesh_id(x, y, z, core):
    return ((lax.rem(z, 2) * 4 + y) * 2 + core, lax.div(z, 2) * 4 + x)


def token_share(x, y, z, core):
    ctx, ulys = mesh_id(x, y, z, core)
    return ctx * 8 + ulys


def kernel(rand_in, q_in, k_in, v_in, w_in, out,
           kb, vb0, vb1, qb, pb, va, vp, ob, att, wv, acc,
           own_sem, s1_send, k_recv, v_recv, q_recv, k_up, k_dn, k_far, v_up, v_dn, v_far,
           ring_send, sib_send, sib_recv, ret_send, ret_recv, w_sem, out_sem, row_in, rand):
    ctx, ulys = lax.axis_index("ctx"), lax.axis_index("ulys")
    core = lax.rem(ctx, 2)
    y = lax.rem(lax.div(ctx, 2), 4)
    z = lax.div(ulys, 4) * 2 + lax.div(ctx, 8)
    x = lax.rem(ulys, 4)
    head = y * 4 + x
    z_up, z_dn, z_far = lax.rem(z + 1, 4), lax.rem(z + 3, 4), lax.rem(z + 2, 4)
    up, dn = mesh_id(x, y, z_up, core), mesh_id(x, y, z_dn, core)
    sib = mesh_id(x, y, z, 1 - core)
    vbs = (vb0, vb1)

    def peer(k):
        return lax.rem(x + lax.rem(k, 4), 4), lax.rem(y + lax.div(k, 4), 4)

    def back(k):
        return lax.rem(x + 4 - lax.rem(k, 4), 4), lax.rem(y + 4 - lax.div(k, 4), 4)

    def lanes(h):
        return pl.ds(pl.multiple_of(h * DH, DH), DH)

    def rows(k, zz):
        px, py = peer(k)
        return pl.ds(token_share(px, py, zz, core) * 4, 4)

    def rows_x(g, zz):
        return pl.ds(token_share(lax.rem(g, 2) * 2, lax.rem(y + lax.div(g, 2), 4), zz, core) * 4, 8)

    def shares(k, count=1):
        return pl.ds(pl.multiple_of(k * SHARE, SHARE), count * SHARE)

    def packed(k, count=1):
        return pl.ds(pl.multiple_of(k * DH, DH), count * DH)

    my_rows = rows(0, z)
    own = [
        pltpu.make_async_copy(rand_in, rand, own_sem.at[3]),
        pltpu.make_async_copy(k_in.at[:, :, lanes(head)], kb.at[my_rows], own_sem.at[0]),
        pltpu.make_async_copy(v_in, va, own_sem.at[1]),
        pltpu.make_async_copy(q_in.at[:, lanes(head)], qb.at[shares(0)], own_sem.at[2]),
    ]
    barrier = pltpu.get_barrier_semaphore()
    for device in (up, dn, sib):
        pl.semaphore_signal(barrier, inc=1, device_id=device, device_id_type=MESH)
    for k in (1, 2, 3, 4, 8, 12):
        px, py = back(k)
        pl.semaphore_signal(barrier, inc=1, device_id=mesh_id(px, py, z, core), device_id_type=MESH)
    for copy in own:
        copy.start()
    pl.semaphore_wait(barrier, 9)
    for k in (4, 8, 12):
        px, py = back(k)
        pl.semaphore_signal(row_in, inc=1, device_id=mesh_id(px, py, z, core), device_id_type=MESH)

    def push(src, dst, send, recv, device):
        pltpu.make_async_remote_copy(
            src_ref=src, dst_ref=dst, send_sem=send, recv_sem=recv,
            device_id=device, device_id_type=MESH).start()

    def arrived(piece, sem):
        pltpu.make_async_copy(piece, piece, sem).wait()

    def send_on(side, piece, via, sem, device):
        push(piece, piece, ring_send.at[side, via], sem, device)

    def share_on(side, piece, plane):
        push(piece, piece, sib_send.at[side, plane], sib_recv.at[side, plane], sib)

    def relay(side, low, high, from_low, from_high, to_far, k):
        arrived(low, from_low)

        @pl.when(lax.rem(k, 2) == 0)
        def _():
            send_on(side, low, 2, to_far, up)
        share_on(side, low, 1)
        arrived(high, from_high)

        @pl.when(lax.rem(k, 2) == 1)
        def _():
            send_on(side, high, 3, to_far, dn)
        share_on(side, high, 2)

    def spread_k(k):
        piece = kb.at[rows(k, z)]
        send_on(0, piece, 0, k_up.at[k], up)
        send_on(0, piece, 1, k_dn.at[k], dn)
        share_on(0, piece, 0)

    def relay_k(k):
        relay(0, kb.at[rows(k, z_dn)], kb.at[rows(k, z_up)], k_up.at[k], k_dn.at[k], k_far.at[k], k)

    def last_k(k):
        piece = kb.at[rows(k, z_far)]
        arrived(piece, k_far.at[k])
        share_on(0, piece, 3)

    def spread_v(h, g):
        piece = vbs[h].at[rows_x(g, z)]
        arrived(piece, v_recv.at[h, g])
        send_on(1 + h, piece, 0, v_up.at[h, g], up)
        send_on(1 + h, piece, 1, v_dn.at[h, g], dn)
        share_on(1 + h, piece, 0)

    def relay_v(h, g):
        relay(1 + h, vbs[h].at[rows_x(g, z_dn)], vbs[h].at[rows_x(g, z_up)],
              v_up.at[h, g], v_dn.at[h, g], v_far.at[h, g], g)

    def last_v(h, g):
        piece = vbs[h].at[rows_x(g, z_far)]
        arrived(piece, v_far.at[h, g])
        share_on(1 + h, piece, 3)

    own[1].wait()
    spread_k(0)

    def send_keys(k):
        px, py = back(k)
        push(k_in.at[:, :, lanes(py * 4 + px)], kb.at[my_rows], s1_send.at[0], k_recv.at[k], mesh_id(px, py, z, core))

    for k in (1, 2, 3, 4, 8, 12):
        send_keys(k)
    pl.semaphore_wait(row_in, 3)

    @pl.loop(0, 9)
    def _(n):
        send_keys(5 + lax.div(n, 3) * 4 + lax.rem(n, 3))

    def send_queries():
        @pl.loop(1, 16)
        def _(k):
            px, py = back(k)
            push(q_in.at[:, lanes(py * 4 + px)], qb.at[shares(k)], s1_send.at[1], q_recv, mesh_id(px, py, z, core))

    lane = lax.broadcasted_iota(jnp.int32, (1, DH), 1)
    low_half = lane < DH // 2

    def swap(a):
        return pltpu.roll(a, DH // 2, axis=1)

    def send_values():
        own[2].wait()

        @pl.loop(0, 16)
        def _(h):
            for blk in range(4):
                top = va[blk * BLK:blk * BLK + 32, lanes(h)].astype(jnp.float32)
                bottom = va[blk * BLK + 32:blk * BLK + 64, lanes(h)].astype(jnp.float32)
                vp[0, h, blk] = jnp.where(low_half, top, swap(bottom)).astype(jnp.bfloat16)
                vp[1, h, blk] = jnp.where(low_half, swap(top), bottom).astype(jnp.bfloat16)

        for h in range(2):
            pltpu.make_async_copy(vp.at[h, head], vbs[h].at[my_rows], v_recv.at[h, lax.div(x, 2)]).start()

            @pl.loop(1, 16)
            def _(k):
                px, py = back(k)
                push(vp.at[h, py * 4 + px], vbs[h].at[my_rows], s1_send.at[2 + h], v_recv.at[h, lax.div(k, 4) * 2 + lax.div(x, 2)],
                     mesh_id(px, py, z, core))

    def load_weight():
        for h in range(2):
            @pl.loop(0, 16)
            def _(k):
                px, py = back(k)
                pltpu.make_async_copy(
                    w_in.at[pl.ds(pl.multiple_of((py * 4 + px) * DH + h * 64, 64), 64)],
                    wv.at[h, pl.ds(pl.multiple_of(k * 64, 64), 64)], w_sem.at[h]).start()

    def blocks_of(g):
        found = []
        for i in range(GANG):
            px, py = peer(g * GANG + i)
            first = token_share(px, py, z, core) * 4
            for j in range(4):
                b = first + j
                found.append([
                    lax.rem(b + NB - 1, NB), b, lax.rem(b + 1, NB), 0, 1,
                    rand[0, b], rand[1, b], rand[2, b],
                ])
        return found

    def gang_rows(g, n):
        return pl.ds(pl.multiple_of(g * GANG * SHARE + n * BLK, BLK), BLK)

    def listed_keys(picks):
        blocks = [kb[pick] for pick in picks]
        return jnp.concatenate([b[0:32] for b in blocks] + [b[32:64] for b in blocks], axis=0)

    def weigh(g):
        scores = [
            lax.dot_general(qb[gang_rows(g, n), :], listed_keys(picks), (((1,), (1,)), ((), ())),
                            preferred_element_type=jnp.float32)
            for n, picks in enumerate(blocks_of(g))
        ]
        peaks = [jnp.max(s, axis=-1, keepdims=True) for s in scores]
        lifted = [jnp.exp2((s - peak) * EXP_SCALE) for s, peak in zip(scores, peaks)]
        scales = [1.0 / jnp.sum(e, axis=-1, keepdims=True) for e in lifted]
        for n, (e, scale) in enumerate(zip(lifted, scales)):
            pb[gang_rows(g, n), :] = (e * scale).astype(jnp.bfloat16)

    def attend(h, g):
        sums = []
        for n, picks in enumerate(blocks_of(g)):
            w = pb[gang_rows(g, n), :]
            w = jnp.concatenate([w[:, 0:256], w[:, 256:512]], axis=0)
            listed = jnp.concatenate([vbs[h][pick] for pick in picks], axis=0)
            sums.append(jnp.dot(w, listed, preferred_element_type=jnp.float32))
        outs = []
        for even, odd in zip(sums[0::2], sums[1::2]):
            outs.append(jnp.where(low_half, even[0:64] + swap(even[64:128]), swap(odd[0:64]) + odd[64:128]))
        ob[h, packed(g * GANG, GANG), :] = jnp.concatenate(outs, axis=0).astype(jnp.bfloat16)
        for i in range(GANG):
            k = g * GANG + i
            px, py = peer(k)

            @pl.when(k > 0)
            def _():
                push(ob.at[h, packed(k)], att.at[h, :, lanes(k)], ret_send.at[h], ret_recv.at[h + h * lax.min(lax.div(k, PART), 1)], mesh_id(px, py, z, core))

            @pl.when(k == 0)
            def _():
                pltpu.make_async_copy(ob.at[h, packed(0)], att.at[h, :, pl.ds(0, DH)], ret_recv.at[h]).start()

    span = pl.ds(0, 64)
    half = pl.ds(0, 32)

    def at(i, begin, end):
        return (i >= begin) & (i < end)

    def at_eight(i, begin):
        return (i >= begin) & (i < begin + 8)

    @pl.loop(1, STOP)
    def _(i):
        @pl.when(i < 16)
        def _():
            arrived(kb.at[rows(i, z)], k_recv.at[i])
            spread_k(i)

        @pl.when(i == Q_AT)
        def _():
            send_queries()

        @pl.when(i == PACK_AT)
        def _():
            send_values()

        @pl.when(i == W_AT)
        def _():
            load_weight()

        for h in range(2):
            @pl.when(at_eight(i, V_AT[h]))
            def _():
                spread_v(h, i - V_AT[h])

        @pl.when(at(i, LAG, 16 + LAG))
        def _():
            relay_k(i - LAG)

        for h in range(2):
            @pl.when(at_eight(i, V_AT[h] + V_LAG))
            def _():
                relay_v(h, i - V_AT[h] - V_LAG)

        @pl.when(at(i, LAG_FAR, 16 + LAG_FAR))
        def _():
            last_k(i - LAG_FAR)

        for h in range(2):
            @pl.when(at_eight(i, V_AT[h] + V_FAR))
            def _():
                last_v(h, i - V_AT[h] - V_FAR)

        @pl.when(i == WEIGH_AT - 1)
        def _():
            own[0].wait()
            own[3].wait()
            arrived(qb.at[shares(0, 15)], q_recv)
            for plane in range(4):
                arrived(kb.at[span], sib_recv.at[0, plane])

        @pl.when(at(i, WEIGH_AT, WEIGH_AT + 16 // GANG))
        def _():
            weigh(i - WEIGH_AT)

        @pl.when(i == FIRST_AT - 1)
        def _():
            for plane in range(4):
                arrived(vb0.at[span], sib_recv.at[1, plane])

        @pl.when(at(i, FIRST_AT, FIRST_AT + 16 // GANG))
        def _():
            attend(0, i - FIRST_AT)

    for plane in range(4):
        arrived(vb1.at[span], sib_recv.at[2, plane])

    @pl.loop(0, 16 // GANG)
    def _(g):
        attend(1, g)

    def unpack(h, begin, end):
        for pair in range(begin, end):
            a = att[h, :, 2 * pair * DH:(2 * pair + 1) * DH].astype(jnp.float32)
            b = att[h, :, (2 * pair + 1) * DH:(2 * pair + 2) * DH].astype(jnp.float32)
            cols = slice(h * 1024 + pair * DH, h * 1024 + (pair + 1) * DH)
            va[0:128, cols] = jnp.where(low_half, a, swap(b)).astype(jnp.bfloat16)
            va[128:256, cols] = jnp.where(low_half, swap(a), b).astype(jnp.bfloat16)

    def tile(n):
        return pl.ds(pl.multiple_of(n * TILE_N, TILE_N), TILE_N)

    arrived(wv.at[0], w_sem.at[0])
    arrived(ob.at[0], ret_recv.at[0])
    unpack(0, 0, 8)

    @pl.loop(0, D // TILE_N)
    def _(n):
        acc[:, tile(n)] = jnp.dot(va[:, 0:1024], wv[0, :, tile(n)], preferred_element_type=jnp.float32)

    arrived(wv.at[1], w_sem.at[1])
    arrived(ob.at[1, packed(0, PART)], ret_recv.at[1])
    unpack(1, 0, PART // 2)

    @pl.loop(0, D // TILE_N)
    def _(n):
        acc[:, tile(n)] += jnp.dot(va[:, 1024:1024 + PART * 64], wv[1, 0:PART * 64, tile(n)], preferred_element_type=jnp.float32)

    arrived(ob.at[1, packed(0, 16 - PART)], ret_recv.at[2])
    unpack(1, PART // 2, 8)

    @pl.loop(0, D // TILE_N)
    def _(n):
        total = acc[:, tile(n)] + jnp.dot(va[:, 1024 + PART * 64:2048], wv[1, PART * 64:1024, tile(n)], preferred_element_type=jnp.float32)
        total = total.astype(jnp.bfloat16)
        done = jnp.concatenate([total[0:64], total[128:192], total[64:128], total[192:256]], axis=0)
        pb[shares(n), :] = done
        pltpu.make_async_copy(pb.at[shares(n)], out.at[:, tile(n)], out_sem).start()

    for i in range(2):
        arrived(ob.at[0, packed(0, 15)], ret_send.at[i])
        arrived(qb.at[shares(0, 15)], s1_send.at[i])
        arrived(ob.at[0, packed(0, 15)], s1_send.at[2 + i])
    for side, buf in enumerate((kb, vb0, vb1)):
        for i in range(2):
            arrived(buf.at[span], ring_send.at[side, i])
        for i in range(2, 4):
            arrived(buf.at[half], ring_send.at[side, i])
        for i in range(4):
            arrived(buf.at[span], sib_send.at[side, i])
    arrived(pb.at[shares(0, D // TILE_N)], out_sem)


def shards(queries, keys, values, rand_blocks, out_weight):
    any_spec = pl.BlockSpec(memory_space=pl.ANY)
    hbm = pl.BlockSpec(memory_space=pltpu.HBM)
    dma = pltpu.SemaphoreType.DMA
    return pl.pallas_call(
        kernel,
        out_shape=jax.ShapeDtypeStruct((SHARE, D), jnp.bfloat16),
        in_specs=[hbm] * 5,
        out_specs=any_spec,
        scratch_shapes=[
            pltpu.VMEM((NB, BLK, DH), jnp.bfloat16),
            pltpu.VMEM((NB, BLK // 2, DH), jnp.bfloat16),
            pltpu.VMEM((NB, BLK // 2, DH), jnp.bfloat16),
            pltpu.VMEM((16 * SHARE, DH), jnp.bfloat16),
            pltpu.VMEM((16 * SHARE, 8 * BLK), jnp.bfloat16),
            pltpu.VMEM((SHARE, H * DH), jnp.bfloat16),
            pltpu.VMEM((2, H, 4, BLK // 2, DH), jnp.bfloat16),
            pltpu.VMEM((2, 16 * SHARE // 2, DH), jnp.bfloat16),
            pltpu.VMEM((2, SHARE // 2, H * DH), jnp.bfloat16),
            pltpu.VMEM((2, H * DH // 2, D), jnp.bfloat16),
            pltpu.VMEM((SHARE, D), jnp.float32),
            dma((4,)), dma((4,)), dma((16,)), dma((2, 8)), dma,
            dma((16,)), dma((16,)), dma((16,)), dma((2, 8)), dma((2, 8)), dma((2, 8)),
            dma((3, 4)), dma((3, 4)), dma((3, 4)), dma((2,)), dma((3,)), dma((2,)), dma, pltpu.SemaphoreType.REGULAR,
            pltpu.SMEM((3, NB), jnp.int32),
        ],
        compiler_params=pltpu.CompilerParams(
            collective_id=0, has_side_effects=True, vmem_limit_bytes=VMEM_MIB * 1024 * 1024),
    )(*[pltpu.with_memory_space_constraint(a, pltpu.HBM) for a in (rand_blocks.T, queries, keys.reshape(4, BLK, H * DH), values, out_weight)])


def solution(mesh):
    return jax.shard_map(
        shards,
        mesh=mesh,
        in_specs=(
            P(("ctx", "ulys"), None),
            P(("ctx", "ulys"), None),
            P(("ctx", "ulys"), None),
            P(),
            P(),
        ),
        out_specs=P(("ctx", "ulys"), None),
        check_vma=False,
    )
```

```python
import functools

import jax
import jax.numpy as jnp
from jax import lax
from jax.experimental import pallas as pl
from jax.experimental.pallas import tpu as pltpu
from jax.sharding import PartitionSpec as P

H = 16
DH = 128
D = 4096
BLK = 64
NB = 512
TOKENS = 32768
SHARE = 256
MESH = pl.DeviceIdType.MESH
TILE_N = 512
LAG = 4
LAG_FAR = 9
V_AT = (16, 27)
V_LAG = 4
V_FAR = 8
Q_AT = 4
PACK_AT = 6
W_AT = 10
WEIGH_AT = 25
FIRST_AT = 32
PART = 4
STOP = 43
VMEM_MIB = 47
GANG = 2
EXP_SCALE = (DH ** -0.5) * 1.4426950408889634


def mesh_id(x, y, z, core):
    return ((lax.rem(z, 2) * 4 + y) * 2 + core, lax.div(z, 2) * 4 + x)


def token_share(x, y, z, core):
    ctx, ulys = mesh_id(x, y, z, core)
    return ctx * 8 + ulys


def kernel(rand_in, q_in, k_in, v_in, w_in, out,
           kb, vb0, vb1, qb, pb, va, vp, ob, att, wv, acc,
           own_sem, s1_send, k_recv, v_recv, q_recv, k_up, k_dn, k_far, v_up, v_dn, v_far,
           ring_send, sib_send, sib_recv, ret_send, ret_recv, w_sem, out_sem, row_in, rand):
    ctx, ulys = lax.axis_index("ctx"), lax.axis_index("ulys")
    core = lax.rem(ctx, 2)
    y = lax.rem(lax.div(ctx, 2), 4)
    z = lax.div(ulys, 4) * 2 + lax.div(ctx, 8)
    x = lax.rem(ulys, 4)
    head = y * 4 + x
    z_up, z_dn, z_far = lax.rem(z + 1, 4), lax.rem(z + 3, 4), lax.rem(z + 2, 4)
    up, dn = mesh_id(x, y, z_up, core), mesh_id(x, y, z_dn, core)
    sib = mesh_id(x, y, z, 1 - core)
    vbs = (vb0, vb1)

    def peer(k):
        return lax.rem(x + lax.rem(k, 4), 4), lax.rem(y + lax.div(k, 4), 4)

    def back(k):
        return lax.rem(x + 4 - lax.rem(k, 4), 4), lax.rem(y + 4 - lax.div(k, 4), 4)

    def lanes(h):
        return pl.ds(pl.multiple_of(h * DH, DH), DH)

    def rows(k, zz):
        px, py = peer(k)
        return pl.ds(token_share(px, py, zz, core) * 4, 4)

    def rows_x(g, zz):
        return pl.ds(token_share(lax.rem(g, 2) * 2, lax.rem(y + lax.div(g, 2), 4), zz, core) * 4, 8)

    def shares(k, count=1):
        return pl.ds(pl.multiple_of(k * SHARE, SHARE), count * SHARE)

    def packed(k, count=1):
        return pl.ds(pl.multiple_of(k * DH, DH), count * DH)

    my_rows = rows(0, z)
    own = [
        pltpu.make_async_copy(rand_in, rand, own_sem.at[3]),
        pltpu.make_async_copy(k_in.at[:, :, lanes(head)], kb.at[my_rows], own_sem.at[0]),
        pltpu.make_async_copy(v_in, va, own_sem.at[1]),
        pltpu.make_async_copy(q_in.at[:, lanes(head)], qb.at[shares(0)], own_sem.at[2]),
    ]
    barrier = pltpu.get_barrier_semaphore()
    for device in (up, dn, sib):
        pl.semaphore_signal(barrier, inc=1, device_id=device, device_id_type=MESH)
    for k in (1, 2, 3, 4, 8, 12):
        px, py = back(k)
        pl.semaphore_signal(barrier, inc=1, device_id=mesh_id(px, py, z, core), device_id_type=MESH)
    for copy in own:
        copy.start()
    pl.semaphore_wait(barrier, 9)
    for k in (4, 8, 12):
        px, py = back(k)
        pl.semaphore_signal(row_in, inc=1, device_id=mesh_id(px, py, z, core), device_id_type=MESH)

    def push(src, dst, send, recv, device):
        pltpu.make_async_remote_copy(
            src_ref=src, dst_ref=dst, send_sem=send, recv_sem=recv,
            device_id=device, device_id_type=MESH).start()

    def arrived(piece, sem):
        pltpu.make_async_copy(piece, piece, sem).wait()

    def send_on(side, piece, via, sem, device):
        push(piece, piece, ring_send.at[side, via], sem, device)

    def share_on(side, piece, plane):
        push(piece, piece, sib_send.at[side, plane], sib_recv.at[side, plane], sib)

    def relay(side, low, high, from_low, from_high, to_far, k):
        arrived(low, from_low)

        @pl.when(lax.rem(k, 2) == 0)
        def _():
            send_on(side, low, 2, to_far, up)
        share_on(side, low, 1)
        arrived(high, from_high)

        @pl.when(lax.rem(k, 2) == 1)
        def _():
            send_on(side, high, 3, to_far, dn)
        share_on(side, high, 2)

    def spread_k(k):
        piece = kb.at[rows(k, z)]
        send_on(0, piece, 0, k_up.at[k], up)
        send_on(0, piece, 1, k_dn.at[k], dn)
        share_on(0, piece, 0)

    def relay_k(k):
        relay(0, kb.at[rows(k, z_dn)], kb.at[rows(k, z_up)], k_up.at[k], k_dn.at[k], k_far.at[k], k)

    def last_k(k):
        piece = kb.at[rows(k, z_far)]
        arrived(piece, k_far.at[k])
        share_on(0, piece, 3)

    def spread_v(h, g):
        piece = vbs[h].at[rows_x(g, z)]
        arrived(piece, v_recv.at[h, g])
        send_on(1 + h, piece, 0, v_up.at[h, g], up)
        send_on(1 + h, piece, 1, v_dn.at[h, g], dn)
        share_on(1 + h, piece, 0)

    def relay_v(h, g):
        relay(1 + h, vbs[h].at[rows_x(g, z_dn)], vbs[h].at[rows_x(g, z_up)],
              v_up.at[h, g], v_dn.at[h, g], v_far.at[h, g], g)

    def last_v(h, g):
        piece = vbs[h].at[rows_x(g, z_far)]
        arrived(piece, v_far.at[h, g])
        share_on(1 + h, piece, 3)

    own[1].wait()
    spread_k(0)

    def send_keys(k):
        px, py = back(k)
        push(k_in.at[:, :, lanes(py * 4 + px)], kb.at[my_rows], s1_send.at[0], k_recv.at[k], mesh_id(px, py, z, core))

    for k in (1, 2, 3, 4, 8, 12):
        send_keys(k)
    pl.semaphore_wait(row_in, 3)

    @pl.loop(0, 9)
    def _(n):
        send_keys(5 + lax.div(n, 3) * 4 + lax.rem(n, 3))

    def send_queries():
        @pl.loop(1, 16)
        def _(k):
            px, py = back(k)
            push(q_in.at[:, lanes(py * 4 + px)], qb.at[shares(k)], s1_send.at[1], q_recv, mesh_id(px, py, z, core))

    lane = lax.broadcasted_iota(jnp.int32, (1, DH), 1)
    low_half = lane < DH // 2

    def swap(a):
        return pltpu.roll(a, DH // 2, axis=1)

    def send_values():
        own[2].wait()

        @pl.loop(0, 16)
        def _(h):
            for blk in range(4):
                top = va[blk * BLK:blk * BLK + 32, lanes(h)].astype(jnp.float32)
                bottom = va[blk * BLK + 32:blk * BLK + 64, lanes(h)].astype(jnp.float32)
                vp[0, h, blk] = jnp.where(low_half, top, swap(bottom)).astype(jnp.bfloat16)
                vp[1, h, blk] = jnp.where(low_half, swap(top), bottom).astype(jnp.bfloat16)

        for h in range(2):
            pltpu.make_async_copy(vp.at[h, head], vbs[h].at[my_rows], v_recv.at[h, lax.div(x, 2)]).start()

            @pl.loop(1, 16)
            def _(k):
                px, py = back(k)
                push(vp.at[h, py * 4 + px], vbs[h].at[my_rows], s1_send.at[2 + h], v_recv.at[h, lax.div(k, 4) * 2 + lax.div(x, 2)],
                     mesh_id(px, py, z, core))

    def load_weight():
        for h in range(2):
            @pl.loop(0, 16)
            def _(k):
                px, py = back(k)
                pltpu.make_async_copy(
                    w_in.at[pl.ds(pl.multiple_of((py * 4 + px) * DH + h * 64, 64), 64)],
                    wv.at[h, pl.ds(pl.multiple_of(k * 64, 64), 64)], w_sem.at[h]).start()

    def blocks_of(g):
        found = []
        for i in range(GANG):
            px, py = peer(g * GANG + i)
            first = token_share(px, py, z, core) * 4
            for j in range(4):
                b = first + j
                found.append([
                    lax.rem(b + NB - 1, NB), b, lax.rem(b + 1, NB), 0, 1,
                    rand[0, b], rand[1, b], rand[2, b],
                ])
        return found

    def gang_rows(g, n):
        return pl.ds(pl.multiple_of(g * GANG * SHARE + n * BLK, BLK), BLK)

    def listed_keys(picks):
        blocks = [kb[pick] for pick in picks]
        return jnp.concatenate([b[0:32] for b in blocks] + [b[32:64] for b in blocks], axis=0)

    def weigh(g):
        scores = [
            lax.dot_general(qb[gang_rows(g, n), :], listed_keys(picks), (((1,), (1,)), ((), ())),
                            preferred_element_type=jnp.float32)
            for n, picks in enumerate(blocks_of(g))
        ]
        peaks = [jnp.max(s, axis=-1, keepdims=True) for s in scores]
        lifted = [jnp.exp2((s - peak) * EXP_SCALE) for s, peak in zip(scores, peaks)]
        scales = [1.0 / jnp.sum(e, axis=-1, keepdims=True) for e in lifted]
        for n, (e, scale) in enumerate(zip(lifted, scales)):
            pb[gang_rows(g, n), :] = (e * scale).astype(jnp.bfloat16)

    def attend(h, g):
        sums = []
        for n, picks in enumerate(blocks_of(g)):
            w = pb[gang_rows(g, n), :]
            w = jnp.concatenate([w[:, 0:256], w[:, 256:512]], axis=0)
            listed = jnp.concatenate([vbs[h][pick] for pick in picks], axis=0)
            sums.append(jnp.dot(w, listed, preferred_element_type=jnp.float32))
        outs = []
        for even, odd in zip(sums[0::2], sums[1::2]):
            outs.append(jnp.where(low_half, even[0:64] + swap(even[64:128]), swap(odd[0:64]) + odd[64:128]))
        ob[h, packed(g * GANG, GANG), :] = jnp.concatenate(outs, axis=0).astype(jnp.bfloat16)
        for i in range(GANG):
            k = g * GANG + i
            px, py = peer(k)

            @pl.when(k > 0)
            def _():
                push(ob.at[h, packed(k)], att.at[h, :, lanes(k)], ret_send.at[h], ret_recv.at[h + h * lax.min(lax.div(k, PART), 1)], mesh_id(px, py, z, core))

            @pl.when(k == 0)
            def _():
                pltpu.make_async_copy(ob.at[h, packed(0)], att.at[h, :, pl.ds(0, DH)], ret_recv.at[h]).start()

    span = pl.ds(0, 64)
    half = pl.ds(0, 32)

    def at(i, begin, end):
        return (i >= begin) & (i < end)

    def at_eight(i, begin):
        return (i >= begin) & (i < begin + 8)

    @pl.loop(1, STOP)
    def _(i):
        @pl.when(i < 16)
        def _():
            arrived(kb.at[rows(i, z)], k_recv.at[i])
            spread_k(i)

        @pl.when(i == Q_AT)
        def _():
            send_queries()

        @pl.when(i == PACK_AT)
        def _():
            send_values()

        @pl.when(i == W_AT)
        def _():
            load_weight()

        for h in range(2):
            @pl.when(at_eight(i, V_AT[h]))
            def _():
                spread_v(h, i - V_AT[h])

        @pl.when(at(i, LAG, 16 + LAG))
        def _():
            relay_k(i - LAG)

        for h in range(2):
            @pl.when(at_eight(i, V_AT[h] + V_LAG))
            def _():
                relay_v(h, i - V_AT[h] - V_LAG)

        @pl.when(at(i, LAG_FAR, 16 + LAG_FAR))
        def _():
            last_k(i - LAG_FAR)

        for h in range(2):
            @pl.when(at_eight(i, V_AT[h] + V_FAR))
            def _():
                last_v(h, i - V_AT[h] - V_FAR)

        @pl.when(i == WEIGH_AT - 1)
        def _():
            own[0].wait()
            own[3].wait()
            arrived(qb.at[shares(0, 15)], q_recv)
            for plane in range(4):
                arrived(kb.at[span], sib_recv.at[0, plane])

        @pl.when(at(i, WEIGH_AT, WEIGH_AT + 16 // GANG))
        def _():
            weigh(i - WEIGH_AT)

        @pl.when(i == FIRST_AT - 1)
        def _():
            for plane in range(4):
                arrived(vb0.at[span], sib_recv.at[1, plane])

        @pl.when(at(i, FIRST_AT, FIRST_AT + 16 // GANG))
        def _():
            attend(0, i - FIRST_AT)

    for plane in range(4):
        arrived(vb1.at[span], sib_recv.at[2, plane])

    @pl.loop(0, 16 // GANG)
    def _(g):
        attend(1, g)

    def unpack(h, begin, end):
        for pair in range(begin, end):
            a = att[h, :, 2 * pair * DH:(2 * pair + 1) * DH].astype(jnp.float32)
            b = att[h, :, (2 * pair + 1) * DH:(2 * pair + 2) * DH].astype(jnp.float32)
            cols = slice(h * 1024 + pair * DH, h * 1024 + (pair + 1) * DH)
            va[0:128, cols] = jnp.where(low_half, a, swap(b)).astype(jnp.bfloat16)
            va[128:256, cols] = jnp.where(low_half, swap(a), b).astype(jnp.bfloat16)

    def tile(n):
        return pl.ds(pl.multiple_of(n * TILE_N, TILE_N), TILE_N)

    arrived(wv.at[0], w_sem.at[0])
    arrived(ob.at[0], ret_recv.at[0])
    unpack(0, 0, 8)

    @pl.loop(0, D // TILE_N)
    def _(n):
        acc[:, tile(n)] = jnp.dot(va[:, 0:1024], wv[0, :, tile(n)], preferred_element_type=jnp.float32)

    arrived(wv.at[1], w_sem.at[1])
    arrived(ob.at[1, packed(0, PART)], ret_recv.at[1])
    unpack(1, 0, PART // 2)

    @pl.loop(0, D // TILE_N)
    def _(n):
        acc[:, tile(n)] += jnp.dot(va[:, 1024:1024 + PART * 64], wv[1, 0:PART * 64, tile(n)], preferred_element_type=jnp.float32)

    arrived(ob.at[1, packed(0, 16 - PART)], ret_recv.at[2])
    unpack(1, PART // 2, 8)

    @pl.loop(0, D // TILE_N)
    def _(n):
        total = acc[:, tile(n)] + jnp.dot(va[:, 1024 + PART * 64:2048], wv[1, PART * 64:1024, tile(n)], preferred_element_type=jnp.float32)
        total = total.astype(jnp.bfloat16)
        done = jnp.concatenate([total[0:64], total[128:192], total[64:128], total[192:256]], axis=0)
        pb[shares(n), :] = done
        pltpu.make_async_copy(pb.at[shares(n)], out.at[:, tile(n)], out_sem).start()

    for i in range(2):
        arrived(ob.at[0, packed(0, 15)], ret_send.at[i])
        arrived(qb.at[shares(0, 15)], s1_send.at[i])
        arrived(ob.at[0, packed(0, 15)], s1_send.at[2 + i])
    for side, buf in enumerate((kb, vb0, vb1)):
        for i in range(2):
            arrived(buf.at[span], ring_send.at[side, i])
        for i in range(2, 4):
            arrived(buf.at[half], ring_send.at[side, i])
        for i in range(4):
            arrived(buf.at[span], sib_send.at[side, i])
    arrived(pb.at[shares(0, D // TILE_N)], out_sem)


def shards(queries, keys, values, rand_blocks, out_weight):
    any_spec = pl.BlockSpec(memory_space=pl.ANY)
    hbm = pl.BlockSpec(memory_space=pltpu.HBM)
    dma = pltpu.SemaphoreType.DMA
    return pl.pallas_call(
        kernel,
        out_shape=jax.ShapeDtypeStruct((SHARE, D), jnp.bfloat16),
        in_specs=[hbm] * 5,
        out_specs=any_spec,
        scratch_shapes=[
            pltpu.VMEM((NB, BLK, DH), jnp.bfloat16),
            pltpu.VMEM((NB, BLK // 2, DH), jnp.bfloat16),
            pltpu.VMEM((NB, BLK // 2, DH), jnp.bfloat16),
            pltpu.VMEM((16 * SHARE, DH), jnp.bfloat16),
            pltpu.VMEM((16 * SHARE, 8 * BLK), jnp.bfloat16),
            pltpu.VMEM((SHARE, H * DH), jnp.bfloat16),
            pltpu.VMEM((2, H, 4, BLK // 2, DH), jnp.bfloat16),
            pltpu.VMEM((2, 16 * SHARE // 2, DH), jnp.bfloat16),
            pltpu.VMEM((2, SHARE // 2, H * DH), jnp.bfloat16),
            pltpu.VMEM((2, H * DH // 2, D), jnp.bfloat16),
            pltpu.VMEM((SHARE, D), jnp.float32),
            dma((4,)), dma((4,)), dma((16,)), dma((2, 8)), dma,
            dma((16,)), dma((16,)), dma((16,)), dma((2, 8)), dma((2, 8)), dma((2, 8)),
            dma((3, 4)), dma((3, 4)), dma((3, 4)), dma((2,)), dma((3,)), dma((2,)), dma, pltpu.SemaphoreType.REGULAR,
            pltpu.SMEM((3, NB), jnp.int32),
        ],
        compiler_params=pltpu.CompilerParams(
            collective_id=0, has_side_effects=True, vmem_limit_bytes=VMEM_MIB * 1024 * 1024),
    )(*[pltpu.with_memory_space_constraint(a, pltpu.HBM) for a in (rand_blocks.T, queries, keys.reshape(4, BLK, H * DH), values, out_weight)])


def solution(mesh):
    return jax.shard_map(
        shards,
        mesh=mesh,
        in_specs=(
            P(("ctx", "ulys"), None),
            P(("ctx", "ulys"), None),
            P(("ctx", "ulys"), None),
            P(),
            P(),
        ),
        out_specs=P(("ctx", "ulys"), None),
        check_vma=False,
    )
```
